32 devices in a mesh: grp: 4 (over y, core), seq: 8 (over z, x).
Axes of the slice: x: 2, y: 2, z: 4, core: 2. Of those that a mesh axis runs over, the one named last changes fastest.
Arguments:
- x_prompt: bfloat16 [2048, 768], P(('grp', 'seq')), may hold values from -6 to 6
- x_cont: bfloat16 [64, 256, 768], P(('grp', 'seq')), may hold values from -6 to 6
- thought_pos: int32 [64, 6], P(('grp', 'seq')), may hold values from 0 to 254, all different within a row
- offsets: int32 [64], P(('grp', 'seq')), may hold values from 1 to 512, as said below
- dy_prompt: float32 [2048, 768], P(('grp', 'seq')), may hold values from -6 to 6
- dy_cont: float32 [64, 256, 768], P(('grp', 'seq')), may hold values from -6 to 6
- w_qkv: bfloat16 [2, 768, 2304], P(None, ('grp', 'seq')), may hold values from -0.21875 to 0.21875
- w_out: bfloat16 [2, 768, 768], P(None, ('grp', 'seq')), may hold values from -1.25 to 1.25
- w_fc: bfloat16 [2, 768, 3072], P(None, ('grp', 'seq')), may hold values from -0.21875 to 0.21875
- w_proj: bfloat16 [2, 3072, 768], P(None, ('grp', 'seq')), may hold values from -0.109375 to 0.109375
- ln1_gain: bfloat16 [2, 768], P(None, ('grp', 'seq')), may hold values from 0.5 to 1.5
- ln1_bias: bfloat16 [2, 768], P(None, ('grp', 'seq')), may hold values from -0.59765625 to 0.59765625
- q_bias: bfloat16 [2, 768], P(None, ('grp', 'seq')), may hold values from -0.59765625 to 0.59765625
- v_bias: bfloat16 [2, 768], P(None, ('grp', 'seq')), may hold values from -0.59765625 to 0.59765625
- out_bias: bfloat16 [2, 768], P(None, ('grp', 'seq')), may hold values from -0.59765625 to 0.59765625
- ln2_gain: bfloat16 [2, 768], P(None, ('grp', 'seq')), may hold values from 0.5 to 1.5
- ln2_bias: bfloat16 [2, 768], P(None, ('grp', 'seq')), may hold values from -0.59765625 to 0.59765625
- fc_bias: bfloat16 [2, 3072], P(None, ('grp', 'seq')), may hold values from -0.59765625 to 0.59765625
- proj_bias: bfloat16 [2, 768], P(None, ('grp', 'seq')), may hold values from -0.59765625 to 0.59765625
Outputs:
- y_prompt: bfloat16 [2048, 768], P(('grp', 'seq'))
- y_cont: bfloat16 [64, 256, 768], P(('grp', 'seq'))
- dx_prompt: float32 [2048, 768], P(('grp', 'seq'))
- dx_cont: float32 [64, 256, 768], P(('grp', 'seq'))
- grad_qkv: float32 [2, 768, 2304], P(None, ('grp', 'seq'))
- grad_out: float32 [2, 768, 768], P(None, ('grp', 'seq'))
- grad_fc: float32 [2, 768, 3072], P(None, ('grp', 'seq'))
- grad_proj: float32 [2, 3072, 768], P(None, ('grp', 'seq'))
- grad_ln1_gain: float32 [2, 768], P(None, ('grp', 'seq'))
- grad_ln1_bias: float32 [2, 768], P(None, ('grp', 'seq'))
- grad_q_bias: float32 [2, 768], P(None, ('grp', 'seq'))
- grad_v_bias: float32 [2, 768], P(None, ('grp', 'seq'))
- grad_out_bias: float32 [2, 768], P(None, ('grp', 'seq'))
- grad_ln2_gain: float32 [2, 768], P(None, ('grp', 'seq'))
- grad_ln2_bias: float32 [2, 768], P(None, ('grp', 'seq'))
- grad_fc_bias: float32 [2, 3072], P(None, ('grp', 'seq'))
- grad_proj_bias: float32 [2, 768], P(None, ('grp', 'seq'))
The draws below stay inside these ranges and needn't reach their ends.
Inputs may be any that keep to these rules, and one draw needn't show every extreme that they name: `thought_pos`: each row names 6 different source positions; the thought of source s sits at position s + 1 of the same continuation. `offsets`: in every group some continuation sees all 512 prompt tokens.
All inputs are finite; a program needn't handle non-finite values.
Results may differ from the reference program's by a relative error of at most 0.018.
Values may be sent and summed in bfloat16 or wider, within the bound.
No kernel may reach another device: no remote copies, remote signals or barrier semaphores. Data moves between devices by JAX's collectives and lax.ppermute only.
A program may use at most 512 MiB of HBM per device.

```python
import jax
import jax.numpy as jnp
from jax import lax

D = 768
HEADS = 12
HD = 64
FF = 3072
LAYERS = 2
CL = 256
NTH = 6
GROUPS = 4
PLEN = 512
CPG = 16
CONTS = 64
PTOK = 2048


def draw_offsets(key, part):
    first = jax.random.fold_in(key, 11)
    second = jax.random.fold_in(key, 23)
    values = jax.random.randint(first, (CONTS,), 1, PLEN + 1)
    chosen = jax.random.randint(second, (GROUPS,), 0, CPG)
    slots = jnp.arange(CONTS) % CPG
    picked = jnp.repeat(chosen, CPG)
    return jnp.where(slots == picked, PLEN, values).astype(jnp.int32)


def levels(rng, dims, split, smallest, largest):
    def one(dim, parts):
        steps = jax.random.uniform(jax.random.fold_in(jax.random.fold_in(rng, 6), dim), (parts,), jnp.float32, smallest / len(split), largest / len(split))
        return jnp.repeat(jnp.exp(steps), dims[dim] // parts).reshape((-1,) + (1,) * (len(dims) - dim - 1))

    factor_of = one(*split[0])
    for cut in split[1:]:
        factor_of = factor_of * one(*cut)
    return factor_of


def different_ones(rng, rows, amount, top, lift):
    sequence = jax.random.permutation(jax.random.fold_in(rng, 1), amount)
    pull = sequence
    for power in range(3):
        pull = pull * pull // amount
    pull = pull * lift // amount
    lots = jax.random.randint(jax.random.fold_in(rng, 2), (rows, amount), 0, 4096) + pull
    sure = jax.random.permutation(jax.random.fold_in(rng, 3), rows)[jnp.arange(amount) % rows]
    lots = jnp.where(jnp.arange(rows)[:, None] == sure[None, :], 1 << 14, lots)
    score = lots * amount + jnp.arange(amount)
    return lax.top_k(score.astype(jnp.int32), top)[1].astype(jnp.int32)


def noise(key, shape, scale, bound, shards=(), kind=jnp.bfloat16):
    array = jax.random.normal(key, shape, jnp.float32) * scale
    if len(shards) > 0:
        array = levels(key, shape, shards, -0.22, 0.18) * array
    return jnp.clip(array, min=-bound, max=bound).astype(kind)


def setup_inputs(seed: int = 0) -> dict:
    seeds = jax.random.split(jax.random.key(seed), 20)
    x_prompt = noise(seeds[0], (PTOK, D), 1.0, 6.0, ((0, 32),))
    x_cont = noise(seeds[1], (CONTS, CL, D), 1.0, 6.0, ((0, 32),))
    thought_pos = different_ones(seeds[2], CONTS, CL - 1, NTH, 0)
    offsets = draw_offsets(jax.random.fold_in(seeds[19], 71), 0)
    dy_prompt = noise(seeds[4], (PTOK, D), 1.0, 6.0, ((0, 32),), jnp.float32)
    dy_cont = noise(seeds[5], (CONTS, CL, D), 1.0, 6.0, ((0, 32),), jnp.float32)
    w_qkv = noise(seeds[6], (LAYERS, D, 3 * D), D ** -0.5, 0.21875, ((1, 32),))
    w_out = noise(seeds[7], (LAYERS, D, D), (D // 32) ** -0.5, 1.25, ((1, 32),))
    w_fc = noise(seeds[8], (LAYERS, D, FF), D ** -0.5, 0.21875, ((1, 32),))
    w_proj = noise(seeds[9], (LAYERS, FF, D), FF ** -0.5, 0.109375, ((1, 32),))
    ln1_gain = jnp.clip(1.0 + 0.1 * jax.random.normal(seeds[10], (LAYERS, D), jnp.float32), 0.5, 1.5).astype(jnp.bfloat16)
    ln1_bias = noise(seeds[11], (LAYERS, D), 0.1, 0.59765625, ((1, 32),))
    q_bias = noise(seeds[12], (LAYERS, D), 0.1, 0.59765625, ((1, 32),))
    v_bias = noise(seeds[13], (LAYERS, D), 0.1, 0.59765625, ((1, 32),))
    out_bias = noise(seeds[14], (LAYERS, D), 0.1, 0.59765625, ((1, 32),))
    ln2_gain = jnp.clip(1.0 + 0.1 * jax.random.normal(seeds[15], (LAYERS, D), jnp.float32), 0.5, 1.5).astype(jnp.bfloat16)
    ln2_bias = noise(seeds[16], (LAYERS, D), 0.1, 0.59765625, ((1, 32),))
    fc_bias = noise(seeds[17], (LAYERS, FF), 0.1, 0.59765625, ((1, 32),))
    proj_bias = noise(seeds[18], (LAYERS, D), 0.1, 0.59765625, ((1, 32),))
    return dict(x_prompt=x_prompt, x_cont=x_cont, thought_pos=thought_pos, offsets=offsets, dy_prompt=dy_prompt, dy_cont=dy_cont, w_qkv=w_qkv, w_out=w_out, w_fc=w_fc, w_proj=w_proj, ln1_gain=ln1_gain, ln1_bias=ln1_bias, q_bias=q_bias, v_bias=v_bias, out_bias=out_bias, ln2_gain=ln2_gain, ln2_bias=ln2_bias, fc_bias=fc_bias, proj_bias=proj_bias)


@jax.custom_vjp
def low(v):
    return lax.optimization_barrier(v.astype(jnp.bfloat16)).astype(jnp.float32)

@jax.custom_vjp
def low_back(v):
    return v

def low_keep(v):
    return (low(v), None)

def low_pass(kept, grad):
    return (grad,)

def back_keep(v):
    return (v, None)

def back_low(kept, grad):
    return (low(grad),)
low.defvjp(low_keep, low_pass)
low_back.defvjp(back_keep, back_low)
epsilon = 1e-05
gelu_coeff = 0.7978845608028654
masked_score = -1e+30

def rounded_both(value):
    return low(low_back(value))

def layer_norm(rows, gain, shift):
    centred = rows - lax.optimization_barrier(jnp.mean(rows, -1, keepdims=True))
    spread = lax.optimization_barrier(jnp.mean(centred * centred, -1, keepdims=True))
    return centred * lax.rsqrt(spread + epsilon) * gain + shift

def gelu_tanh(value):
    return 0.5 * value * (1.0 + jnp.tanh(gelu_coeff * (value + 0.044715 * value * value * value)))

def matrix_product(left, right):
    flat = left.reshape(-1, left.shape[-1])
    result = jnp.dot(flat, right, precision=lax.Precision.HIGHEST)
    return result.reshape(left.shape[:-1] + (right.shape[-1],))

def attention(queries, keys, values, visible):
    rows = queries.shape[0]
    query_heads = queries.reshape(rows, HEADS, HD)
    key_heads = keys.reshape(keys.shape[0], HEADS, HD)
    value_heads = values.reshape(values.shape[0], HEADS, HD)
    scores = jnp.einsum('rhe,she->hrs', query_heads, key_heads, precision=lax.Precision.HIGHEST) * 0.125
    scores = low_back(scores)
    scores = jnp.where(visible[None], scores, masked_score)
    shifted = scores - lax.optimization_barrier(jnp.max(scores, -1, keepdims=True))
    expd = jnp.exp(shifted)
    probs = expd / lax.optimization_barrier(jnp.sum(expd, -1, keepdims=True))
    mixed = jnp.einsum('hrs,she->rhe', low(probs), value_heads, precision=lax.Precision.HIGHEST)
    return rounded_both(mixed.reshape(rows, HEADS * HD))

def attention_inputs(weights, rows):
    normed = low(layer_norm(rows, weights[4], weights[5]))
    mixed = matrix_product(normed, weights[0])
    queries = rounded_both(mixed[..., :D] + weights[6])
    keys = rounded_both(mixed[..., D:2 * D])
    values = rounded_both(mixed[..., 2 * D:] + weights[7])
    return (queries, keys, values)

def block_output(weights, rows, mixed):
    after = rows + low_back(matrix_product(mixed, weights[1]) + weights[8])
    normed = low(layer_norm(after, weights[9], weights[10]))
    hidden = low_back(matrix_product(normed, weights[2]) + weights[11])
    active = low(gelu_tanh(hidden))
    return after + low_back(matrix_product(active, weights[3]) + weights[12])

def prompt_layer(weights, rows):
    queries, keys, values = attention_inputs(weights, rows)
    block = min(512, PLEN)
    blocks = PLEN // block
    starts = jnp.arange(blocks, dtype=jnp.int32) * block

    def one_block(args):
        query_block, start = args
        rows_at = start + jnp.arange(block, dtype=jnp.int32)
        visible = rows_at[:, None] >= jnp.arange(PLEN, dtype=jnp.int32)[None, :]
        return attention(query_block, keys, values, visible)
    mixed = lax.map(jax.checkpoint(one_block), (queries.reshape(blocks, block, D), starts))
    return (block_output(weights, rows, mixed.reshape(PLEN, D)), keys, values)

def cont_layer(weights, rows, prompt_keys, prompt_values, seen):
    queries, keys, values = attention_inputs(weights, rows)
    causal = jnp.arange(CL, dtype=jnp.int32)[:, None] >= jnp.arange(CL, dtype=jnp.int32)[None, :]

    def one_cont(args):
        query_c, key_c, value_c, offset = args
        prompt_seen = jnp.broadcast_to(jnp.arange(PLEN, dtype=jnp.int32)[None, :] < offset, (CL, PLEN))
        visible = jnp.concatenate([prompt_seen, causal], 1)
        return attention(query_c, jnp.concatenate([prompt_keys, key_c], 0), jnp.concatenate([prompt_values, value_c], 0), visible)
    mixed = lax.map(jax.checkpoint(one_cont), (queries, keys, values, seen))
    return block_output(weights, rows, mixed)

def group_forward(weights, prompt_rows, cont_rows, sources, seen):
    rows = prompt_rows
    pairs = []
    for layer in range(LAYERS):
        layer_weights = tuple((part[layer] for part in weights))
        rows, keys, values = prompt_layer(layer_weights, rows)
        pairs.append((keys, values))
    current = cont_rows
    for layer in range(LAYERS):
        layer_weights = tuple((part[layer] for part in weights))
        current = cont_layer(layer_weights, current, pairs[layer][0], pairs[layer][1], seen)
    shifted = jnp.concatenate([jnp.zeros_like(current[:, :1]), current[:, :-1]], 1)
    marked = jnp.any(sources[:, :, None] + 1 == jnp.arange(CL, dtype=jnp.int32)[None, None, :], 1)[:, :, None]
    current = jnp.where(marked, shifted, cont_rows)
    for layer in range(LAYERS):
        layer_weights = tuple((part[layer] for part in weights))
        current = cont_layer(layer_weights, current, pairs[layer][0], pairs[layer][1], seen)
    return (rows, current)

def reference(x_prompt, x_cont, thought_pos, offsets, dy_prompt, dy_cont, w_qkv, w_out, w_fc, w_proj, ln1_gain, ln1_bias, q_bias, v_bias, out_bias, ln2_gain, ln2_bias, fc_bias, proj_bias):
    weights = tuple((part.astype(jnp.float32) for part in (w_qkv, w_out, w_fc, w_proj, ln1_gain, ln1_bias, q_bias, v_bias, out_bias, ln2_gain, ln2_bias, fc_bias, proj_bias)))
    prompt_rows = x_prompt.astype(jnp.float32).reshape(GROUPS, PLEN, D)
    cont_rows = x_cont.astype(jnp.float32).reshape(GROUPS, CPG, CL, D)
    sources = thought_pos.reshape(GROUPS, CPG, NTH)
    seen = offsets.reshape(GROUPS, CPG)

    def forward(weights, prompt_rows, cont_rows):
        rounded = tuple((low(part) for part in weights))

        def one_group(args):
            return group_forward(rounded, args[0], args[1], args[2], args[3])
        return lax.map(jax.checkpoint(one_group), (prompt_rows, cont_rows, sources, seen))
    outputs, pullback = jax.vjp(forward, weights, prompt_rows, cont_rows)
    grads, grad_prompt, grad_cont = pullback((dy_prompt.astype(jnp.float32).reshape(GROUPS, PLEN, D), dy_cont.astype(jnp.float32).reshape(GROUPS, CPG, CL, D)))
    return (outputs[0].reshape(PTOK, D).astype(jnp.bfloat16), outputs[1].reshape(CONTS, CL, D).astype(jnp.bfloat16), grad_prompt.reshape(PTOK, D), grad_cont.reshape(CONTS, CL, D), grads[0], grads[1], grads[2], grads[3], grads[4], grads[5], grads[6], grads[7], grads[8], grads[9], grads[10], grads[11], grads[12])
```

```python
import functools

import jax
import jax.numpy as jnp
from jax import lax
from jax.experimental import pallas as pl
from jax.experimental.pallas import tpu as pltpu
from jax.sharding import PartitionSpec as P

HEADS = 12
LAYERS = 2
epsilon = 1e-05
score_scale = 0.125
gelu_coeff = 0.7978845608028654
gelu_cubic = 0.044715
masked_score = -1e30
ALL = ("grp", "seq")
bf16 = jnp.bfloat16
f32 = jnp.float32


def nn(left, right):
    return lax.dot_general(left, right, (((1,), (0,)), ((), ())), preferred_element_type=f32)


def nt(left, right):
    return lax.dot_general(left, right, (((1,), (1,)), ((), ())), preferred_element_type=f32)


def tn(left, right):
    return lax.dot_general(left, right, (((0,), (0,)), ((), ())), preferred_element_type=f32)


def head_split(pair, width):
    lane = lax.broadcasted_iota(jnp.int32, pair.shape, 1)
    zero = jnp.zeros_like(pair)
    return jnp.where(lane < width, pair, zero), jnp.where(lane >= width, pair, zero)


def attend_kernel(seen_ref, q_ref, k_ref, v_ref, pk_ref, pv_ref, o_ref, lse_ref, *, width):
    offset = seen_ref[pl.program_id(0)]
    length, plen = q_ref.shape[0], pk_ref.shape[0]
    queries = head_split(q_ref[...] * bf16(score_scale), width)
    prompt_keys, own_keys = pk_ref[...], k_ref[...]
    prompt_values, own_values = pv_ref[...].T, v_ref[...].T
    visible = lax.broadcasted_iota(jnp.int32, (plen, length), 0) < offset
    causal = lax.broadcasted_iota(jnp.int32, (length, length), 0) <= lax.broadcasted_iota(
        jnp.int32, (length, length), 1
    )
    mixed = []
    for head in range(2):
        rows = slice(head * width, (head + 1) * width)
        prompt_scores = jnp.where(visible, nt(prompt_keys, queries[head]), masked_score)
        own_scores = jnp.where(causal, nt(own_keys, queries[head]), masked_score)
        top = jnp.maximum(
            jnp.max(prompt_scores, 0, keepdims=True), jnp.max(own_scores, 0, keepdims=True)
        )
        prompt_exp = jnp.exp(prompt_scores - top)
        own_exp = jnp.exp(own_scores - top)
        total = jnp.sum(prompt_exp, 0, keepdims=True) + jnp.sum(own_exp, 0, keepdims=True)
        summed = nn(prompt_values[rows], prompt_exp.astype(bf16)) + nn(
            own_values[rows], own_exp.astype(bf16)
        )
        mixed.append(summed / total)
        lse_ref[0, head : head + 1, :] = top + jnp.log(total)
    o_ref[...] = jnp.concatenate(mixed, 0).T.astype(bf16)


def attend(seen, qkv, pqkv):
    rows, width = qkv.shape[0], qkv.shape[1] // 3
    count, plen = seen.shape[0], pqkv.shape[0]
    length, head_width, pairs = rows // count, width // HEADS, HEADS // 2
    lanes = 2 * head_width

    def part(size, which, own):
        return pl.BlockSpec(
            (size, lanes), lambda c, p, s: (c if own else 0, p + which * pairs)
        )

    return pl.pallas_call(
        functools.partial(attend_kernel, width=head_width),
        grid_spec=pltpu.PrefetchScalarGridSpec(
            num_scalar_prefetch=1,
            grid=(count, pairs),
            in_specs=[
                part(length, 0, True),
                part(length, 1, True),
                part(length, 2, True),
                part(plen, 1, False),
                part(plen, 2, False),
            ],
            out_specs=[
                part(length, 0, True),
                pl.BlockSpec((1, 2, length), lambda c, p, s: (c * pairs + p, 0, 0)),
            ],
        ),
        out_shape=[
            jax.ShapeDtypeStruct((rows, width), bf16),
            jax.ShapeDtypeStruct((count * pairs, 2, length), f32),
        ],
        cost_estimate=pl.CostEstimate(
            flops=4 * rows * (plen + length) * width,
            bytes_accessed=2 * (4 * rows + 2 * plen) * width,
            transcendentals=rows * (plen + length) * HEADS,
        ),
        name="attend",
    )(seen, qkv, qkv, qkv, pqkv, pqkv)


def attend_back_kernel(
    seen_ref,
    q_ref,
    k_ref,
    v_ref,
    pk_ref,
    pv_ref,
    o_ref,
    lse_ref,
    do_ref,
    carry_ref,
    dqkv_ref,
    dpkv_ref,
    *,
    width,
    pairs,
):
    cont, pair = pl.program_id(0), pl.program_id(1)
    offset = seen_ref[cont]
    length, plen = q_ref.shape[0], pk_ref.shape[0]
    lanes = 2 * width
    queries = head_split(q_ref[...] * bf16(score_scale), width)
    grad = do_ref[...]
    grads = head_split(grad, width)
    prompt_keys, own_keys = pk_ref[...], k_ref[...]
    prompt_values, own_values = pv_ref[...], v_ref[...]
    prompt_turned, own_turned = prompt_keys.T, own_keys.T
    product = (grad.astype(f32) * o_ref[...].astype(f32)).T
    visible = lax.broadcasted_iota(jnp.int32, (plen, length), 0) < offset
    causal = lax.broadcasted_iota(jnp.int32, (length, length), 0) <= lax.broadcasted_iota(
        jnp.int32, (length, length), 1
    )
    dq = []
    dk = dv = dpk = dpv = 0.0
    for head in range(2):
        rows = slice(head * width, (head + 1) * width)
        query, grad_head = queries[head], grads[head]
        delta = jnp.sum(product[rows], 0, keepdims=True)
        lse = lse_ref[0, head : head + 1, :]
        prompt_p = jnp.exp(jnp.where(visible, nt(prompt_keys, query), masked_score) - lse)
        own_p = jnp.exp(jnp.where(causal, nt(own_keys, query), masked_score) - lse)
        prompt_ds = (prompt_p * (nt(prompt_values, grad_head) - delta)).astype(bf16)
        own_ds = (own_p * (nt(own_values, grad_head) - delta)).astype(bf16)
        dpv += nn(prompt_p.astype(bf16), grad_head)
        dv += nn(own_p.astype(bf16), grad_head)
        dpk += nn(prompt_ds, query)
        dk += nn(own_ds, query)
        dq.append(nn(prompt_turned[rows], prompt_ds) + nn(own_turned[rows], own_ds))
    first = pl.multiple_of(pair * lanes, lanes)
    columns = [pl.ds(first + number * pairs * lanes, lanes) for number in range(3)]
    dqkv_ref[:, columns[0]] = (jnp.concatenate(dq, 0).T * score_scale).astype(bf16)
    dqkv_ref[:, columns[1]] = dk.astype(bf16)
    dqkv_ref[:, columns[2]] = dv.astype(bf16)

    @pl.when(cont == 0)
    def _():
        dpkv_ref[:, columns[0]] = carry_ref[:, columns[0]] + dpk
        dpkv_ref[:, columns[1]] = carry_ref[:, columns[1]] + dpv

    @pl.when(cont > 0)
    def _():
        dpkv_ref[:, columns[0]] += dpk
        dpkv_ref[:, columns[1]] += dpv


def attend_back(seen, qkv, pqkv, o, lse, do, carry):
    rows, width = qkv.shape[0], qkv.shape[1] // 3
    count, plen = seen.shape[0], pqkv.shape[0]
    length, head_width, pairs = rows // count, width // HEADS, HEADS // 2
    lanes = 2 * head_width

    def part(size, which, own):
        return pl.BlockSpec(
            (size, lanes), lambda c, p, s: (c if own else 0, p + which * pairs)
        )

    whole = pl.BlockSpec((plen, 2 * width), lambda c, p, s: (0, 0))
    return pl.pallas_call(
        functools.partial(attend_back_kernel, width=head_width, pairs=pairs),
        grid_spec=pltpu.PrefetchScalarGridSpec(
            num_scalar_prefetch=1,
            grid=(count, pairs),
            in_specs=[
                part(length, 0, True),
                part(length, 1, True),
                part(length, 2, True),
                part(plen, 1, False),
                part(plen, 2, False),
                part(length, 0, True),
                pl.BlockSpec((1, 2, length), lambda c, p, s: (c * pairs + p, 0, 0)),
                part(length, 0, True),
                whole,
            ],
            out_specs=[pl.BlockSpec((length, 3 * width), lambda c, p, s: (c, 0)), whole],
        ),
        out_shape=[
            jax.ShapeDtypeStruct((rows, 3 * width), bf16),
            jax.ShapeDtypeStruct((plen, 2 * width), f32),
        ],
        cost_estimate=pl.CostEstimate(
            flops=10 * rows * (plen + length) * width,
            bytes_accessed=2 * (8 * rows + 10 * plen) * width,
            transcendentals=rows * (plen + length) * HEADS,
        ),
        name="attend_back",
    )(seen, qkv, qkv, qkv, pqkv, pqkv, o, lse, do, carry)


def stacked_heads(pair, width):
    return jnp.concatenate(head_split(pair, width), 0)


def unstacked(block, width):
    rows = block.shape[0] // 2
    lane = lax.broadcasted_iota(jnp.int32, (rows, block.shape[1]), 1)
    return jnp.where(lane < width, block[:rows], block[rows:])


def prompt_scores(place_ref, q_ref, k_ref, width):
    rows, plen = q_ref.shape[0], k_ref.shape[0]
    queries = stacked_heads(q_ref[...] * bf16(score_scale), width)
    column = lax.broadcasted_iota(jnp.int32, (plen, 2 * rows), 1)
    query_row = jnp.where(column < rows, column, column - rows) + place_ref[0] * rows
    visible = lax.broadcasted_iota(jnp.int32, (plen, 2 * rows), 0) <= query_row
    return queries, jnp.where(visible, nt(k_ref[...], queries), masked_score)


def prompt_kernel(place_ref, q_ref, k_ref, v_ref, o_ref, lse_ref, *, width):
    queries, scores = prompt_scores(place_ref, q_ref, k_ref, width)
    top = jnp.max(scores, 0, keepdims=True)
    expd = jnp.exp(scores - top)
    total = jnp.sum(expd, 0, keepdims=True)
    mixed = nn(v_ref[...].T, expd.astype(bf16)) / total
    o_ref[...] = unstacked(mixed.T, width).astype(bf16)
    lse_ref[0] = top + jnp.log(total)


def prompt_specs(rows, plen, pairs, lanes):
    return [
        pl.BlockSpec((rows, lanes), lambda p, s: (s[0], p)),
        pl.BlockSpec((plen, lanes), lambda p, s: (0, p + pairs)),
        pl.BlockSpec((plen, lanes), lambda p, s: (0, p + 2 * pairs)),
    ]


def prompt_attend(place, pqkv, rows):
    plen, width = pqkv.shape[0], pqkv.shape[1] // 3
    pairs, head_width = HEADS // 2, width // HEADS
    lanes = 2 * head_width
    return pl.pallas_call(
        functools.partial(prompt_kernel, width=head_width),
        grid_spec=pltpu.PrefetchScalarGridSpec(
            num_scalar_prefetch=1,
            grid=(pairs,),
            in_specs=prompt_specs(rows, plen, pairs, lanes),
            out_specs=[
                pl.BlockSpec((rows, lanes), lambda p, s: (0, p)),
                pl.BlockSpec((1, 1, 2 * rows), lambda p, s: (p, 0, 0)),
            ],
        ),
        out_shape=[
            jax.ShapeDtypeStruct((rows, width), bf16),
            jax.ShapeDtypeStruct((pairs, 1, 2 * rows), f32),
        ],
        cost_estimate=pl.CostEstimate(
            flops=4 * rows * plen * width,
            bytes_accessed=6 * plen * width,
            transcendentals=rows * plen * HEADS,
        ),
        name="prompt_attend",
    )(place, pqkv, pqkv, pqkv)


def prompt_back_kernel(
    place_ref, q_ref, k_ref, v_ref, o_ref, lse_ref, do_ref, carry_k, carry_v, dq_ref, dk_ref, dv_ref, *, width
):
    queries, scores = prompt_scores(place_ref, q_ref, k_ref, width)
    grads = stacked_heads(do_ref[...], width)
    output = o_ref[...]
    product = grads.astype(f32) * jnp.concatenate([output, output], 0).astype(f32)
    delta = jnp.sum(product.T, 0, keepdims=True)
    probs = jnp.exp(scores - lse_ref[0])
    ds = (probs * (nt(v_ref[...], grads) - delta)).astype(bf16)
    dv_ref[...] = carry_v[...] + nn(probs.astype(bf16), grads)
    dk_ref[...] = carry_k[...] + nn(ds, queries)
    turned = nn(k_ref[...].T, ds) * score_scale
    dq_ref[...] = unstacked(turned.T, width).astype(bf16)


def prompt_back(place, pqkv, o, lse, do, carry):
    rows, plen, width = o.shape[0], pqkv.shape[0], pqkv.shape[1] // 3
    pairs, head_width = HEADS // 2, width // HEADS
    lanes = 2 * head_width
    own = pl.BlockSpec((rows, lanes), lambda p, s: (0, p))
    keys = pl.BlockSpec((plen, lanes), lambda p, s: (0, p))
    values = pl.BlockSpec((plen, lanes), lambda p, s: (0, p + pairs))
    total = jax.ShapeDtypeStruct((plen, width), f32)
    dq, dk, dv = pl.pallas_call(
        functools.partial(prompt_back_kernel, width=head_width),
        grid_spec=pltpu.PrefetchScalarGridSpec(
            num_scalar_prefetch=1,
            grid=(pairs,),
            in_specs=prompt_specs(rows, plen, pairs, lanes)
            + [own, pl.BlockSpec((1, 1, 2 * rows), lambda p, s: (p, 0, 0)), own, keys, values],
            out_specs=[own, keys, keys],
        ),
        out_shape=[jax.ShapeDtypeStruct((rows, width), bf16), total, total],
        cost_estimate=pl.CostEstimate(
            flops=10 * rows * plen * width,
            bytes_accessed=24 * plen * width,
            transcendentals=rows * plen * HEADS,
        ),
        name="prompt_back",
    )(place, pqkv, pqkv, pqkv, o, lse, do, carry, carry)
    return dq, dk, dv


def normalised(rows):
    centred = rows - jnp.mean(rows, -1, keepdims=True)
    scale = lax.rsqrt(jnp.mean(centred * centred, -1, keepdims=True) + epsilon)
    return centred * scale, scale


def norm(rows, gain, shift):
    return (normalised(rows)[0] * gain + shift).astype(bf16)


def norm_back(rows, gain, grad):
    unit, scale = normalised(rows)
    inner = grad * gain
    spread = inner - jnp.mean(inner, -1, keepdims=True) - unit * jnp.mean(inner * unit, -1, keepdims=True)
    return spread * scale, jnp.sum(grad * unit, 0), jnp.sum(grad, 0)


def gelu(value):
    return 0.5 * value * (1.0 + jnp.tanh(gelu_coeff * (value + gelu_cubic * value * value * value)))


def gelu_slope(value):
    square = value * value
    bent = jnp.tanh(gelu_coeff * value * (1.0 + gelu_cubic * square))
    inner = gelu_coeff * (1.0 + 3.0 * gelu_cubic * square)
    return 0.5 * (1.0 + bent) + 0.5 * value * (1.0 - bent * bent) * inner


def column_sums(block):
    return jnp.sum(block.astype(f32), 0)


def block_output(w, rows, mixed):
    after = rows + nn(mixed, w["out"]) + w["out_bias"]
    normed = norm(after, w["ln2_gain"], w["ln2_bias"])
    hidden = nn(normed, w["fc"]) + w["fc_bias"]
    active = gelu(hidden).astype(bf16)
    result = after + nn(active, w["proj"]) + w["proj_bias"]
    return result, (after, normed, hidden.astype(bf16), active)


def output_backward(w, kept, grad_rows):
    after, normed, hidden, active = kept
    dz = grad_rows.astype(bf16)
    du = (nt(dz, w["proj"]) * gelu_slope(hidden.astype(f32))).astype(bf16)
    grad_in, gain, shift = norm_back(after, w["ln2_gain"], nt(du, w["fc"]))
    grad_after = grad_in + grad_rows
    da = grad_after.astype(bf16)
    do = nt(da, w["out"]).astype(bf16)
    return grad_after, do, (dz, du, da), (gain, shift)


SMALL = (
    "ln1_gain",
    "ln1_bias",
    "q_bias",
    "v_bias",
    "out_bias",
    "ln2_gain",
    "ln2_bias",
    "proj_bias",
    "fc_bias",
)


def body(
    x_prompt,
    x_cont,
    thought_pos,
    offsets,
    dy_prompt,
    dy_cont,
    w_qkv,
    w_out,
    w_fc,
    w_proj,
    ln1_gain,
    ln1_bias,
    q_bias,
    v_bias,
    out_bias,
    ln2_gain,
    ln2_bias,
    fc_bias,
    proj_bias,
):
    count, length, width = x_cont.shape
    rows = count * length
    prompt_dev = x_prompt.shape[0]
    plen = prompt_dev * lax.axis_size("seq")
    devices = lax.axis_size("grp") * lax.axis_size("seq")
    place = lax.axis_index("seq")
    place_ref = place.astype(jnp.int32).reshape(1)
    vectors = dict(
        ln1_gain=ln1_gain,
        ln1_bias=ln1_bias,
        q_bias=q_bias,
        v_bias=v_bias,
        out_bias=out_bias,
        ln2_gain=ln2_gain,
        ln2_bias=ln2_bias,
        proj_bias=proj_bias,
        fc_bias=fc_bias,
    )
    out_rows = w_out.shape[1]
    sizes = [vectors[name].shape[1] for name in SMALL]
    x_all = lax.all_gather(x_prompt, "seq", axis=0, tiled=True)

    weights = []
    for layer in range(LAYERS):
        flat = jnp.concatenate([vectors[name][layer] for name in SMALL])
        extra = jnp.pad(flat, (0, 8 * width - flat.shape[0])).reshape(8, width)
        pack = lax.all_gather(jnp.concatenate([w_out[layer], extra], 0), ALL, axis=0)
        w = dict(out=pack[:, :out_rows].reshape(width, width))
        share = pack[:, out_rows:].reshape(devices, 8 * width)
        first = 0
        for name, size in zip(SMALL, sizes):
            w[name] = share[:, first : first + size].reshape(devices * size).astype(f32)
            first += size
        for name, part in (("qkv", w_qkv), ("fc", w_fc), ("proj", w_proj)):
            w[name] = lax.all_gather(part[layer], ALL, axis=0, tiled=True)
        w["qkv_bias"] = jnp.concatenate([w["q_bias"], jnp.zeros((width,), f32), w["v_bias"]])
        weights.append(w)

    def project(w, normed):
        return (nn(normed, w["qkv"]) + w["qkv_bias"]).astype(bf16)

    prompt_rows = x_prompt.astype(f32)
    prompt_states = []
    for layer in range(LAYERS):
        w = weights[layer]
        if layer == 0:
            all_normed = norm(x_all.astype(f32), w["ln1_gain"], w["ln1_bias"])
        else:
            all_normed = lax.all_gather(
                norm(prompt_rows, w["ln1_gain"], w["ln1_bias"]), "seq", axis=0, tiled=True
            )
        pqkv = project(w, all_normed)
        mixed, lse = prompt_attend(place_ref, pqkv, prompt_dev)
        result, kept = block_output(w, prompt_rows, mixed)
        prompt_states.append((prompt_rows, all_normed, pqkv, mixed, lse, kept))
        prompt_rows = result
    prompt_out = prompt_rows

    def pass_forward(current):
        states = []
        for layer in range(LAYERS):
            w = weights[layer]
            normed = norm(current, w["ln1_gain"], w["ln1_bias"])
            qkv = project(w, normed)
            mixed, lse = attend(offsets, qkv, prompt_states[layer][2])
            result, kept = block_output(w, current, mixed)
            states.append((current, normed, qkv, mixed, lse, kept))
            current = result
        return current, states

    inputs = x_cont.astype(f32)
    latent, latent_states = pass_forward(inputs.reshape(rows, width))
    latent = latent.reshape(count, length, width)
    shifted = jnp.concatenate([jnp.zeros((count, 1, width), f32), latent[:, :-1]], 1)
    marked = jnp.any(
        thought_pos[:, :, None] + 1 == lax.broadcasted_iota(jnp.int32, (1, 1, length), 2), 1
    )[:, :, None]
    current, language_states = pass_forward(jnp.where(marked, shifted, inputs).reshape(rows, width))
    cont_out = current.reshape(count, length, width).astype(bf16)

    pieces = [[] for layer in range(LAYERS)]
    small = [[] for layer in range(LAYERS)]
    carries = [jnp.zeros((plen, 2 * width), f32) for layer in range(LAYERS)]

    def layer_backward(layer, state, grad):
        w = weights[layer]
        before, normed, qkv, mixed, lse, kept = state
        grad_after, do, (dz, du, da), ln2 = output_backward(w, kept, grad)
        dqkv, carries[layer] = attend_back(
            offsets, qkv, prompt_states[layer][2], mixed, lse, do, carries[layer]
        )
        grad_in, gain, shift = norm_back(before, w["ln1_gain"], nt(dqkv, w["qkv"]))
        pieces[layer].append((normed, dqkv, mixed, da, kept[1], du, kept[3], dz))
        small[layer].append((gain, shift) + ln2)
        return grad_after + grad_in

    grad = dy_cont.reshape(rows, width)
    for layer in reversed(range(LAYERS)):
        grad = layer_backward(layer, language_states[layer], grad)
    grad_mixed_in = grad.reshape(count, length, width)
    grad = jnp.concatenate(
        [jnp.where(marked, grad_mixed_in, 0.0)[:, 1:], jnp.zeros((count, 1, width), f32)], 1
    ).reshape(rows, width)
    prompt_grad = dy_prompt
    shares = []
    for layer in reversed(range(LAYERS)):
        w = weights[layer]
        grad = layer_backward(layer, latent_states[layer], grad)
        before, normed, pqkv, mixed, lse, kept = prompt_states[layer]
        grad_after, do, (dz, du, da), ln2 = output_backward(w, kept, prompt_grad)
        dq, dk, dv = prompt_back(place_ref, pqkv, mixed, lse, do, carries[layer])
        dq_all = lax.dynamic_update_slice(
            jnp.zeros((plen, width), bf16), dq, (place * prompt_dev, 0)
        )
        dqkv = jnp.concatenate([dq_all, dk.astype(bf16), dv.astype(bf16)], 1)
        grad_normed = lax.psum_scatter(
            nt(dqkv, w["qkv"]).astype(bf16), "seq", scatter_dimension=0, tiled=True
        ).astype(f32)
        grad_in, gain, shift = norm_back(before, w["ln1_gain"], grad_normed)
        prompt_grad = grad_after + grad_in
        pieces[layer].append((normed, dqkv, mixed, da, kept[1], du, kept[3], dz))
        small[layer].append((gain, shift) + ln2)

        joined = [jnp.concatenate(parts, 0) for parts in zip(*pieces[layer])]
        gain1, shift1, gain2, shift2 = [sum(parts) for parts in zip(*small[layer])]
        qkv_sums = column_sums(joined[1])
        vector_grads = dict(
            ln1_gain=gain1,
            ln1_bias=shift1,
            q_bias=qkv_sums[:width],
            v_bias=qkv_sums[2 * width :],
            out_bias=column_sums(joined[3]),
            ln2_gain=gain2,
            ln2_bias=shift2,
            proj_bias=column_sums(joined[7]),
            fc_bias=column_sums(joined[5]),
        )
        flat = jnp.concatenate(
            [
                vector_grads[name].reshape(devices, size)
                for name, size in zip(SMALL, sizes)
            ],
            1,
        )
        extra = jnp.pad(flat, ((0, 0), (0, 8 * width - flat.shape[1]))).reshape(devices, 8, width)
        pack = jnp.concatenate(
            [tn(joined[2], joined[3]).reshape(devices, out_rows, width), extra], 1
        ).astype(bf16)
        totals = [
            lax.psum_scatter(part.astype(bf16), ALL, scatter_dimension=0, tiled=True).astype(f32)
            for part in (
                tn(joined[6], joined[7]),
                tn(joined[4], joined[5]),
                pack,
                tn(joined[0], joined[1]),
            )
        ]
        share = totals[2].reshape(out_rows + 8, width)
        result = dict(proj=totals[0], fc=totals[1], out=share[:out_rows], qkv=totals[3])
        share = share[out_rows:].reshape(8 * width)
        first = 0
        for name, size in zip(SMALL, sizes):
            result[name] = share[first : first + size]
            first += size
        shares.append(result)
    shares.reverse()
    grad_cont = jnp.where(marked, 0.0, grad_mixed_in) + grad.reshape(count, length, width)
    names = ("qkv", "out", "fc", "proj") + (
        "ln1_gain",
        "ln1_bias",
        "q_bias",
        "v_bias",
        "out_bias",
        "ln2_gain",
        "ln2_bias",
        "fc_bias",
        "proj_bias",
    )
    return (prompt_out.astype(bf16), cont_out, prompt_grad, grad_cont) + tuple(
        jnp.stack([shares[layer][name] for layer in range(LAYERS)]) for name in names
    )


def solution(mesh):
    row, cube, matrix, vector = (
        P(ALL, None),
        P(ALL, None, None),
        P(None, ALL, None),
        P(None, ALL),
    )
    return jax.shard_map(
        body,
        mesh=mesh,
        in_specs=(row, cube, row, P(ALL), row, cube) + (matrix,) * 4 + (vector,) * 9,
        out_specs=(row, cube, row, cube) + (matrix,) * 4 + (vector,) * 9,
        check_vma=False,
    )
```

```python
import functools

import jax
import jax.numpy as jnp
from jax import lax
from jax.experimental import pallas as pl
from jax.experimental.pallas import tpu as pltpu
from jax.sharding import PartitionSpec as P

HEADS = 12
LAYERS = 2
epsilon = 1e-05
score_scale = 0.125
gelu_coeff = 0.7978845608028654
gelu_cubic = 0.044715
masked_score = -1e30
ALL = ("grp", "seq")
bf16 = jnp.bfloat16
f32 = jnp.float32


def nn(left, right):
    return lax.dot_general(left, right, (((1,), (0,)), ((), ())), preferred_element_type=f32)


def nt(left, right):
    return lax.dot_general(left, right, (((1,), (1,)), ((), ())), preferred_element_type=f32)


def tn(left, right):
    return lax.dot_general(left, right, (((0,), (0,)), ((), ())), preferred_element_type=f32)


def head_split(pair, width):
    lane = lax.broadcasted_iota(jnp.int32, pair.shape, 1)
    zero = jnp.zeros_like(pair)
    return jnp.where(lane < width, pair, zero), jnp.where(lane >= width, pair, zero)


def attend_kernel(seen_ref, q_ref, k_ref, v_ref, pk_ref, pv_ref, o_ref, lse_ref, *, width):
    offset = seen_ref[pl.program_id(0)]
    length, plen = q_ref.shape[0], pk_ref.shape[0]
    queries = head_split(q_ref[...] * bf16(score_scale), width)
    prompt_keys, own_keys = pk_ref[...], k_ref[...]
    prompt_values, own_values = pv_ref[...].T, v_ref[...].T
    visible = lax.broadcasted_iota(jnp.int32, (plen, length), 0) < offset
    causal = lax.broadcasted_iota(jnp.int32, (length, length), 0) <= lax.broadcasted_iota(
        jnp.int32, (length, length), 1
    )
    mixed = []
    for head in range(2):
        rows = slice(head * width, (head + 1) * width)
        prompt_scores = jnp.where(visible, nt(prompt_keys, queries[head]), masked_score)
        own_scores = jnp.where(causal, nt(own_keys, queries[head]), masked_score)
        top = jnp.maximum(
            jnp.max(prompt_scores, 0, keepdims=True), jnp.max(own_scores, 0, keepdims=True)
        )
        prompt_exp = jnp.exp(prompt_scores - top)
        own_exp = jnp.exp(own_scores - top)
        total = jnp.sum(prompt_exp, 0, keepdims=True) + jnp.sum(own_exp, 0, keepdims=True)
        summed = nn(prompt_values[rows], prompt_exp.astype(bf16)) + nn(
            own_values[rows], own_exp.astype(bf16)
        )
        mixed.append(summed / total)
        lse_ref[0, head : head + 1, :] = top + jnp.log(total)
    o_ref[...] = jnp.concatenate(mixed, 0).T.astype(bf16)


def attend(seen, qkv, pqkv):
    rows, width = qkv.shape[0], qkv.shape[1] // 3
    count, plen = seen.shape[0], pqkv.shape[0]
    length, head_width, pairs = rows // count, width // HEADS, HEADS // 2
    lanes = 2 * head_width

    def part(size, which, own):
        return pl.BlockSpec(
            (size, lanes), lambda c, p, s: (c if own else 0, p + which * pairs)
        )

    return pl.pallas_call(
        functools.partial(attend_kernel, width=head_width),
        grid_spec=pltpu.PrefetchScalarGridSpec(
            num_scalar_prefetch=1,
            grid=(count, pairs),
            in_specs=[
                part(length, 0, True),
                part(length, 1, True),
                part(length, 2, True),
                part(plen, 1, False),
                part(plen, 2, False),
            ],
            out_specs=[
                part(length, 0, True),
                pl.BlockSpec((1, 2, length), lambda c, p, s: (c * pairs + p, 0, 0)),
            ],
        ),
        out_shape=[
            jax.ShapeDtypeStruct((rows, width), bf16),
            jax.ShapeDtypeStruct((count * pairs, 2, length), f32),
        ],
        cost_estimate=pl.CostEstimate(
            flops=4 * rows * (plen + length) * width,
            bytes_accessed=2 * (4 * rows + 2 * plen) * width,
            transcendentals=rows * (plen + length) * HEADS,
        ),
        name="attend",
    )(seen, qkv, qkv, qkv, pqkv, pqkv)


def attend_back_kernel(
    seen_ref,
    q_ref,
    k_ref,
    v_ref,
    pk_ref,
    pv_ref,
    o_ref,
    lse_ref,
    do_ref,
    carry_ref,
    dqkv_ref,
    dpkv_ref,
    *,
    width,
    pairs,
):
    cont, pair = pl.program_id(0), pl.program_id(1)
    offset = seen_ref[cont]
    length, plen = q_ref.shape[0], pk_ref.shape[0]
    lanes = 2 * width
    queries = head_split(q_ref[...] * bf16(score_scale), width)
    grad = do_ref[...]
    grads = head_split(grad, width)
    prompt_keys, own_keys = pk_ref[...], k_ref[...]
    prompt_values, own_values = pv_ref[...], v_ref[...]
    prompt_turned, own_turned = prompt_keys.T, own_keys.T
    product = (grad.astype(f32) * o_ref[...].astype(f32)).T
    visible = lax.broadcasted_iota(jnp.int32, (plen, length), 0) < offset
    causal = lax.broadcasted_iota(jnp.int32, (length, length), 0) <= lax.broadcasted_iota(
        jnp.int32, (length, length), 1
    )
    dq = []
    dk = dv = dpk = dpv = 0.0
    for head in range(2):
        rows = slice(head * width, (head + 1) * width)
        query, grad_head = queries[head], grads[head]
        delta = jnp.sum(product[rows], 0, keepdims=True)
        lse = lse_ref[0, head : head + 1, :]
        prompt_p = jnp.exp(jnp.where(visible, nt(prompt_keys, query), masked_score) - lse)
        own_p = jnp.exp(jnp.where(causal, nt(own_keys, query), masked_score) - lse)
        prompt_ds = (prompt_p * (nt(prompt_values, grad_head) - delta)).astype(bf16)
        own_ds = (own_p * (nt(own_values, grad_head) - delta)).astype(bf16)
        dpv += nn(prompt_p.astype(bf16), grad_head)
        dv += nn(own_p.astype(bf16), grad_head)
        dpk += nn(prompt_ds, query)
        dk += nn(own_ds, query)
        dq.append(nn(prompt_turned[rows], prompt_ds) + nn(own_turned[rows], own_ds))
    first = pl.multiple_of(pair * lanes, lanes)
    columns = [pl.ds(first + number * pairs * lanes, lanes) for number in range(3)]
    dqkv_ref[:, columns[0]] = (jnp.concatenate(dq, 0).T * score_scale).astype(bf16)
    dqkv_ref[:, columns[1]] = dk.astype(bf16)
    dqkv_ref[:, columns[2]] = dv.astype(bf16)

    @pl.when(cont == 0)
    def _():
        dpkv_ref[:, columns[0]] = carry_ref[:, columns[0]] + dpk
        dpkv_ref[:, columns[1]] = carry_ref[:, columns[1]] + dpv

    @pl.when(cont > 0)
    def _():
        dpkv_ref[:, columns[0]] += dpk
        dpkv_ref[:, columns[1]] += dpv


def attend_back(seen, qkv, pqkv, o, lse, do, carry):
    rows, width = qkv.shape[0], qkv.shape[1] // 3
    count, plen = seen.shape[0], pqkv.shape[0]
    length, head_width, pairs = rows // count, width // HEADS, HEADS // 2
    lanes = 2 * head_width

    def part(size, which, own):
        return pl.BlockSpec(
            (size, lanes), lambda c, p, s: (c if own else 0, p + which * pairs)
        )

    whole = pl.BlockSpec((plen, 2 * width), lambda c, p, s: (0, 0))
    return pl.pallas_call(
        functools.partial(attend_back_kernel, width=head_width, pairs=pairs),
        grid_spec=pltpu.PrefetchScalarGridSpec(
            num_scalar_prefetch=1,
            grid=(count, pairs),
            in_specs=[
                part(length, 0, True),
                part(length, 1, True),
                part(length, 2, True),
                part(plen, 1, False),
                part(plen, 2, False),
                part(length, 0, True),
                pl.BlockSpec((1, 2, length), lambda c, p, s: (c * pairs + p, 0, 0)),
                part(length, 0, True),
                whole,
            ],
            out_specs=[pl.BlockSpec((length, 3 * width), lambda c, p, s: (c, 0)), whole],
        ),
        out_shape=[
            jax.ShapeDtypeStruct((rows, 3 * width), bf16),
            jax.ShapeDtypeStruct((plen, 2 * width), f32),
        ],
        cost_estimate=pl.CostEstimate(
            flops=10 * rows * (plen + length) * width,
            bytes_accessed=2 * (8 * rows + 10 * plen) * width,
            transcendentals=rows * (plen + length) * HEADS,
        ),
        name="attend_back",
    )(seen, qkv, qkv, qkv, pqkv, pqkv, o, lse, do, carry)


def stacked_heads(pair, width):
    return jnp.concatenate(head_split(pair, width), 0)


def unstacked(block, width):
    rows = block.shape[0] // 2
    lane = lax.broadcasted_iota(jnp.int32, (rows, block.shape[1]), 1)
    return jnp.where(lane < width, block[:rows], block[rows:])


def prompt_scores(place_ref, q_ref, k_ref, width):
    rows, plen = q_ref.shape[0], k_ref.shape[0]
    queries = stacked_heads(q_ref[...] * bf16(score_scale), width)
    column = lax.broadcasted_iota(jnp.int32, (plen, 2 * rows), 1)
    query_row = jnp.where(column < rows, column, column - rows) + place_ref[0] * rows
    visible = lax.broadcasted_iota(jnp.int32, (plen, 2 * rows), 0) <= query_row
    return queries, jnp.where(visible, nt(k_ref[...], queries), masked_score)


def prompt_kernel(place_ref, q_ref, k_ref, v_ref, o_ref, lse_ref, *, width):
    queries, scores = prompt_scores(place_ref, q_ref, k_ref, width)
    top = jnp.max(scores, 0, keepdims=True)
    expd = jnp.exp(scores - top)
    total = jnp.sum(expd, 0, keepdims=True)
    mixed = nn(v_ref[...].T, expd.astype(bf16)) / total
    o_ref[...] = unstacked(mixed.T, width).astype(bf16)
    lse_ref[0] = top + jnp.log(total)


def prompt_specs(rows, plen, pairs, lanes):
    return [
        pl.BlockSpec((rows, lanes), lambda p, s: (s[0], p)),
        pl.BlockSpec((plen, lanes), lambda p, s: (0, p + pairs)),
        pl.BlockSpec((plen, lanes), lambda p, s: (0, p + 2 * pairs)),
    ]


def prompt_attend(place, pqkv, rows):
    plen, width = pqkv.shape[0], pqkv.shape[1] // 3
    pairs, head_width = HEADS // 2, width // HEADS
    lanes = 2 * head_width
    return pl.pallas_call(
        functools.partial(prompt_kernel, width=head_width),
        grid_spec=pltpu.PrefetchScalarGridSpec(
            num_scalar_prefetch=1,
            grid=(pairs,),
            in_specs=prompt_specs(rows, plen, pairs, lanes),
            out_specs=[
                pl.BlockSpec((rows, lanes), lambda p, s: (0, p)),
                pl.BlockSpec((1, 1, 2 * rows), lambda p, s: (p, 0, 0)),
            ],
        ),
        out_shape=[
            jax.ShapeDtypeStruct((rows, width), bf16),
            jax.ShapeDtypeStruct((pairs, 1, 2 * rows), f32),
        ],
        cost_estimate=pl.CostEstimate(
            flops=4 * rows * plen * width,
            bytes_accessed=6 * plen * width,
            transcendentals=rows * plen * HEADS,
        ),
        name="prompt_attend",
    )(place, pqkv, pqkv, pqkv)


def prompt_back_kernel(
    place_ref, q_ref, k_ref, v_ref, o_ref, lse_ref, do_ref, carry_k, carry_v, dq_ref, dk_ref, dv_ref, *, width
):
    queries, scores = prompt_scores(place_ref, q_ref, k_ref, width)
    grads = stacked_heads(do_ref[...], width)
    output = o_ref[...]
    product = grads.astype(f32) * jnp.concatenate([output, output], 0).astype(f32)
    delta = jnp.sum(product.T, 0, keepdims=True)
    probs = jnp.exp(scores - lse_ref[0])
    ds = (probs * (nt(v_ref[...], grads) - delta)).astype(bf16)
    dv_ref[...] = carry_v[...] + nn(probs.astype(bf16), grads)
    dk_ref[...] = carry_k[...] + nn(ds, queries)
    turned = nn(k_ref[...].T, ds) * score_scale
    dq_ref[...] = unstacked(turned.T, width).astype(bf16)


def prompt_back(place, pqkv, o, lse, do, carry):
    rows, plen, width = o.shape[0], pqkv.shape[0], pqkv.shape[1] // 3
    pairs, head_width = HEADS // 2, width // HEADS
    lanes = 2 * head_width
    own = pl.BlockSpec((rows, lanes), lambda p, s: (0, p))
    keys = pl.BlockSpec((plen, lanes), lambda p, s: (0, p))
    values = pl.BlockSpec((plen, lanes), lambda p, s: (0, p + pairs))
    total = jax.ShapeDtypeStruct((plen, width), f32)
    dq, dk, dv = pl.pallas_call(
        functools.partial(prompt_back_kernel, width=head_width),
        grid_spec=pltpu.PrefetchScalarGridSpec(
            num_scalar_prefetch=1,
            grid=(pairs,),
            in_specs=prompt_specs(rows, plen, pairs, lanes)
            + [own, pl.BlockSpec((1, 1, 2 * rows), lambda p, s: (p, 0, 0)), own, keys, values],
            out_specs=[own, keys, keys],
        ),
        out_shape=[jax.ShapeDtypeStruct((rows, width), bf16), total, total],
        cost_estimate=pl.CostEstimate(
            flops=10 * rows * plen * width,
            bytes_accessed=24 * plen * width,
            transcendentals=rows * plen * HEADS,
        ),
        name="prompt_back",
    )(place, pqkv, pqkv, pqkv, o, lse, do, carry, carry)
    return dq, dk, dv


def normalised(rows):
    centred = rows - jnp.mean(rows, -1, keepdims=True)
    scale = lax.rsqrt(jnp.mean(centred * centred, -1, keepdims=True) + epsilon)
    return centred * scale, scale


def norm(rows, gain, shift):
    return (normalised(rows)[0] * gain + shift).astype(bf16)


def norm_back(rows, gain, grad):
    unit, scale = normalised(rows)
    inner = grad * gain
    spread = inner - jnp.mean(inner, -1, keepdims=True) - unit * jnp.mean(inner * unit, -1, keepdims=True)
    return spread * scale, jnp.sum(grad * unit, 0), jnp.sum(grad, 0)


def gelu(value):
    return 0.5 * value * (1.0 + jnp.tanh(gelu_coeff * (value + gelu_cubic * value * value * value)))


def gelu_slope(value):
    square = value * value
    bent = jnp.tanh(gelu_coeff * value * (1.0 + gelu_cubic * square))
    inner = gelu_coeff * (1.0 + 3.0 * gelu_cubic * square)
    return 0.5 * (1.0 + bent) + 0.5 * value * (1.0 - bent * bent) * inner


def column_sums(block):
    return jnp.sum(block.astype(f32), 0)


def block_output(w, rows, mixed):
    after = rows + nn(mixed, w["out"]) + w["out_bias"]
    normed = norm(after, w["ln2_gain"], w["ln2_bias"])
    hidden = nn(normed, w["fc"]) + w["fc_bias"]
    active = gelu(hidden).astype(bf16)
    result = after + nn(active, w["proj"]) + w["proj_bias"]
    return result, (after, normed, hidden.astype(bf16), active)


def output_backward(w, kept, grad_rows):
    after, normed, hidden, active = kept
    dz = grad_rows.astype(bf16)
    du = (nt(dz, w["proj"]) * gelu_slope(hidden.astype(f32))).astype(bf16)
    grad_in, gain, shift = norm_back(after, w["ln2_gain"], nt(du, w["fc"]))
    grad_after = grad_in + grad_rows
    da = grad_after.astype(bf16)
    do = nt(da, w["out"]).astype(bf16)
    return grad_after, do, (dz, du, da), (gain, shift)


def swap(value, code, axes, total):
    return lax.ppermute(value, axes, [(i, i ^ code) for i in range(total)])


def lay_kernel(place_ref, *refs, codes):
    out_ref, sems = refs[-2], refs[-1]
    copies = []
    for ref, group in zip(refs, codes):
        for number, code in enumerate(group):
            copies.append(
                pltpu.make_async_copy(
                    ref.at[number], out_ref.at[place_ref[0] ^ code], sems.at[len(copies)]
                )
            )
            copies[-1].start()
    for copy in copies:
        copy.wait()


def lay_out(place, pieces, codes, name):
    total = sum(len(group) for group in codes)
    shape = (total,) + pieces[0].shape[1:]
    return pl.pallas_call(
        functools.partial(lay_kernel, codes=codes),
        in_specs=[pl.BlockSpec(memory_space=pltpu.SMEM)]
        + [pl.BlockSpec(memory_space=pl.ANY)] * len(pieces),
        out_specs=pl.BlockSpec(shape, lambda: (0, 0, 0)),
        out_shape=jax.ShapeDtypeStruct(shape, pieces[0].dtype),
        scratch_shapes=[pltpu.SemaphoreType.DMA((total,))],
        cost_estimate=pl.CostEstimate(
            flops=0, bytes_accessed=4 * shape[0] * shape[1] * shape[2], transcendentals=0
        ),
        name=name,
    )(place, *pieces)


def gather_blocks(part, place, x_first, tree):
    if not tree:
        return lax.all_gather(part, ALL, axis=0)
    own = part[None]
    base = jnp.concatenate([own] + [swap(own, code, ALL, 32) for code in (2, 4, 6)], 0)
    first, second = (1, 16) if x_first else (16, 1)
    pieces = [base, swap(base, first, ALL, 32)]
    pieces += [swap(piece, second, ALL, 32) for piece in pieces]
    pieces += [swap(piece, 8, ALL, 32) for piece in pieces]
    starts = [0, first, second, first | second]
    starts += [start | 8 for start in starts]
    codes = tuple(tuple(start | code for code in (0, 2, 4, 6)) for start in starts)
    return lay_out(place, pieces, codes, "lay_weights")


def gather_rows(part, place, tree):
    if not tree:
        return lax.all_gather(part, "seq", axis=0, tiled=True)
    own = part[None]
    pieces = [own] + [swap(own, code, "seq", 8) for code in range(1, 8)]
    codes = tuple((code,) for code in range(8))
    return lay_out(place, pieces, codes, "lay_rows").reshape(8 * part.shape[0], part.shape[1])


def scatter_rows(block, place, tree):
    if not tree:
        return lax.psum_scatter(block, "seq", scatter_dimension=0, tiled=True).astype(f32)
    rows = block.shape[0] // 8
    total = lax.dynamic_slice_in_dim(block, place * rows, rows, 0).astype(f32)
    for code in range(1, 8):
        piece = lax.dynamic_slice_in_dim(block, (place ^ code) * rows, rows, 0)
        total = total + swap(piece, code, "seq", 8).astype(f32)
    return total


SMALL = (
    "ln1_gain",
    "ln1_bias",
    "q_bias",
    "v_bias",
    "out_bias",
    "ln2_gain",
    "ln2_bias",
    "proj_bias",
    "fc_bias",
)


def body(
    x_prompt,
    x_cont,
    thought_pos,
    offsets,
    dy_prompt,
    dy_cont,
    w_qkv,
    w_out,
    w_fc,
    w_proj,
    ln1_gain,
    ln1_bias,
    q_bias,
    v_bias,
    out_bias,
    ln2_gain,
    ln2_bias,
    fc_bias,
    proj_bias,
):
    count, length, width = x_cont.shape
    rows = count * length
    prompt_dev = x_prompt.shape[0]
    plen = prompt_dev * lax.axis_size("seq")
    devices = lax.axis_size("grp") * lax.axis_size("seq")
    place = lax.axis_index("seq")
    place_ref = place.astype(jnp.int32).reshape(1)
    vectors = dict(
        ln1_gain=ln1_gain,
        ln1_bias=ln1_bias,
        q_bias=q_bias,
        v_bias=v_bias,
        out_bias=out_bias,
        ln2_gain=ln2_gain,
        ln2_bias=ln2_bias,
        proj_bias=proj_bias,
        fc_bias=fc_bias,
    )
    out_rows = w_out.shape[1]
    sizes = [vectors[name].shape[1] for name in SMALL]
    tree = (
        lax.axis_size("grp") == 4 and lax.axis_size("seq") == 8 and out_rows % 8 == 0 and prompt_dev % 16 == 0
    )
    flat_ref = (lax.axis_index("grp") * lax.axis_size("seq") + place).astype(jnp.int32).reshape(1)
    x_all = gather_rows(x_prompt, place_ref, tree)

    weights = []
    for layer in range(LAYERS):
        flat = jnp.concatenate([vectors[name][layer] for name in SMALL])
        extra = jnp.pad(flat, (0, 8 * width - flat.shape[0])).reshape(8, width)
        pack = gather_blocks(jnp.concatenate([w_out[layer], extra], 0), flat_ref, False, tree)
        w = dict(out=pack[:, :out_rows].reshape(width, width))
        share = pack[:, out_rows:].reshape(devices, 8 * width)
        first = 0
        for name, size in zip(SMALL, sizes):
            w[name] = share[:, first : first + size].reshape(devices * size).astype(f32)
            first += size
        for name, part, x_first in (("qkv", w_qkv, False), ("fc", w_fc, True), ("proj", w_proj, layer == 0)):
            w[name] = gather_blocks(part[layer], flat_ref, x_first, tree).reshape(-1, part.shape[2])
        w["qkv_bias"] = jnp.concatenate([w["q_bias"], jnp.zeros((width,), f32), w["v_bias"]])
        weights.append(w)

    def project(w, normed):
        return (nn(normed, w["qkv"]) + w["qkv_bias"]).astype(bf16)

    prompt_rows = x_prompt.astype(f32)
    prompt_states = []
    for layer in range(LAYERS):
        w = weights[layer]
        if layer == 0:
            all_normed = norm(x_all.astype(f32), w["ln1_gain"], w["ln1_bias"])
        else:
            all_normed = gather_rows(norm(prompt_rows, w["ln1_gain"], w["ln1_bias"]), place_ref, tree)
        pqkv = project(w, all_normed)
        mixed, lse = prompt_attend(place_ref, pqkv, prompt_dev)
        result, kept = block_output(w, prompt_rows, mixed)
        prompt_states.append((prompt_rows, all_normed, pqkv, mixed, lse, kept))
        prompt_rows = result
    prompt_out = prompt_rows

    def pass_forward(current):
        states = []
        for layer in range(LAYERS):
            w = weights[layer]
            normed = norm(current, w["ln1_gain"], w["ln1_bias"])
            qkv = project(w, normed)
            mixed, lse = attend(offsets, qkv, prompt_states[layer][2])
            result, kept = block_output(w, current, mixed)
            states.append((current, normed, qkv, mixed, lse, kept))
            current = result
        return current, states

    inputs = x_cont.astype(f32)
    latent, latent_states = pass_forward(inputs.reshape(rows, width))
    latent = latent.reshape(count, length, width)
    shifted = jnp.concatenate([jnp.zeros((count, 1, width), f32), latent[:, :-1]], 1)
    marked = jnp.any(
        thought_pos[:, :, None] + 1 == lax.broadcasted_iota(jnp.int32, (1, 1, length), 2), 1
    )[:, :, None]
    current, language_states = pass_forward(jnp.where(marked, shifted, inputs).reshape(rows, width))
    cont_out = current.reshape(count, length, width).astype(bf16)

    pieces = [[] for layer in range(LAYERS)]
    small = [[] for layer in range(LAYERS)]
    carries = [jnp.zeros((plen, 2 * width), f32) for layer in range(LAYERS)]

    def layer_backward(layer, state, grad):
        w = weights[layer]
        before, normed, qkv, mixed, lse, kept = state
        grad_after, do, (dz, du, da), ln2 = output_backward(w, kept, grad)
        dqkv, carries[layer] = attend_back(
            offsets, qkv, prompt_states[layer][2], mixed, lse, do, carries[layer]
        )
        grad_in, gain, shift = norm_back(before, w["ln1_gain"], nt(dqkv, w["qkv"]))
        pieces[layer].append((normed, dqkv, mixed, da, kept[1], du, kept[3], dz))
        small[layer].append((gain, shift) + ln2)
        return grad_after + grad_in

    grad = dy_cont.reshape(rows, width)
    for layer in reversed(range(LAYERS)):
        grad = layer_backward(layer, language_states[layer], grad)
    grad_mixed_in = grad.reshape(count, length, width)
    grad = jnp.concatenate(
        [jnp.where(marked, grad_mixed_in, 0.0)[:, 1:], jnp.zeros((count, 1, width), f32)], 1
    ).reshape(rows, width)
    prompt_grad = dy_prompt
    shares = []
    for layer in reversed(range(LAYERS)):
        w = weights[layer]
        grad = layer_backward(layer, latent_states[layer], grad)
        before, normed, pqkv, mixed, lse, kept = prompt_states[layer]
        grad_after, do, (dz, du, da), ln2 = output_backward(w, kept, prompt_grad)
        dq, dk, dv = prompt_back(place_ref, pqkv, mixed, lse, do, carries[layer])
        dq_all = lax.dynamic_update_slice(
            jnp.zeros((plen, width), bf16), dq, (place * prompt_dev, 0)
        )
        dqkv = jnp.concatenate([dq_all, dk.astype(bf16), dv.astype(bf16)], 1)
        grad_normed = scatter_rows(nt(dqkv, w["qkv"]).astype(bf16), place, tree)
        grad_in, gain, shift = norm_back(before, w["ln1_gain"], grad_normed)
        prompt_grad = grad_after + grad_in
        pieces[layer].append((normed, dqkv, mixed, da, kept[1], du, kept[3], dz))
        small[layer].append((gain, shift) + ln2)

        joined = [jnp.concatenate(parts, 0) for parts in zip(*pieces[layer])]
        gain1, shift1, gain2, shift2 = [sum(parts) for parts in zip(*small[layer])]
        qkv_sums = column_sums(joined[1])
        vector_grads = dict(
            ln1_gain=gain1,
            ln1_bias=shift1,
            q_bias=qkv_sums[:width],
            v_bias=qkv_sums[2 * width :],
            out_bias=column_sums(joined[3]),
            ln2_gain=gain2,
            ln2_bias=shift2,
            proj_bias=column_sums(joined[7]),
            fc_bias=column_sums(joined[5]),
        )
        flat = jnp.concatenate(
            [
                vector_grads[name].reshape(devices, size)
                for name, size in zip(SMALL, sizes)
            ],
            1,
        )
        small_lanes = -(-flat.shape[1] // (128 * out_rows)) * 128
        extra = jnp.pad(flat, ((0, 0), (0, out_rows * small_lanes - flat.shape[1])))
        mlp = tn(joined[6], joined[7]).astype(bf16).reshape(devices, -1, out_rows, width)
        pack = jnp.concatenate(
            [
                tn(joined[0], joined[1]).astype(bf16).reshape(devices, out_rows, -1),
                tn(joined[4], joined[5]).astype(bf16).reshape(devices, out_rows, -1),
                tn(joined[2], joined[3]).astype(bf16).reshape(devices, out_rows, width),
            ]
            + [mlp[:, number] for number in range(mlp.shape[1])]
            + [extra.astype(bf16).reshape(devices, out_rows, small_lanes)],
            2,
        )
        total = lax.psum_scatter(pack, ALL, scatter_dimension=0, tiled=True).astype(f32)[0]
        result = dict(
            qkv=total[:, : 3 * width],
            fc=total[:, 3 * width : 7 * width],
            out=total[:, 7 * width : 8 * width],
            proj=jnp.concatenate(
                [total[:, (8 + number) * width : (9 + number) * width] for number in range(mlp.shape[1])], 0
            ),
        )
        share = total[:, (8 + mlp.shape[1]) * width :].reshape(-1)
        first = 0
        for name, size in zip(SMALL, sizes):
            result[name] = share[first : first + size]
            first += size
        shares.append(result)
    shares.reverse()
    grad_cont = jnp.where(marked, 0.0, grad_mixed_in) + grad.reshape(count, length, width)
    names = ("qkv", "out", "fc", "proj") + (
        "ln1_gain",
        "ln1_bias",
        "q_bias",
        "v_bias",
        "out_bias",
        "ln2_gain",
        "ln2_bias",
        "fc_bias",
        "proj_bias",
    )
    return (prompt_out.astype(bf16), cont_out, prompt_grad, grad_cont) + tuple(
        jnp.stack([shares[layer][name] for layer in range(LAYERS)]) for name in names
    )


def solution(mesh):
    row, cube, matrix, vector = (
        P(ALL, None),
        P(ALL, None, None),
        P(None, ALL, None),
        P(None, ALL),
    )
    return jax.shard_map(
        body,
        mesh=mesh,
        in_specs=(row, cube, row, P(ALL), row, cube) + (matrix,) * 4 + (vector,) * 9,
        out_specs=(row, cube, row, cube) + (matrix,) * 4 + (vector,) * 9,
        check_vma=False,
    )
```

```python
import functools

import jax
import jax.numpy as jnp
from jax import lax
from jax.experimental import pallas as pl
from jax.experimental.pallas import tpu as pltpu
from jax.sharding import PartitionSpec as P

HEADS = 12
LAYERS = 2
epsilon = 1e-05
score_scale = 0.125
gelu_coeff = 0.7978845608028654
gelu_cubic = 0.044715
masked_score = -1e30
ALL = ("grp", "seq")
bf16 = jnp.bfloat16
f32 = jnp.float32


def nn(left, right):
    return lax.dot_general(left, right, (((1,), (0,)), ((), ())), preferred_element_type=f32)


def nt(left, right):
    return lax.dot_general(left, right, (((1,), (1,)), ((), ())), preferred_element_type=f32)


def tn(left, right):
    return lax.dot_general(left, right, (((0,), (0,)), ((), ())), preferred_element_type=f32)


def head_split(pair, width):
    lane = lax.broadcasted_iota(jnp.int32, pair.shape, 1)
    zero = jnp.zeros_like(pair)
    return jnp.where(lane < width, pair, zero), jnp.where(lane >= width, pair, zero)


def attend_kernel(seen_ref, q_ref, k_ref, v_ref, pk_ref, pv_ref, o_ref, lse_ref, *, width):
    offset = seen_ref[pl.program_id(0)]
    length, plen = q_ref.shape[0], pk_ref.shape[0]
    queries = head_split(q_ref[...] * bf16(score_scale), width)
    prompt_keys, own_keys = pk_ref[...], k_ref[...]
    prompt_values, own_values = pv_ref[...].T, v_ref[...].T
    visible = lax.broadcasted_iota(jnp.int32, (plen, length), 0) < offset
    causal = lax.broadcasted_iota(jnp.int32, (length, length), 0) <= lax.broadcasted_iota(
        jnp.int32, (length, length), 1
    )
    mixed = []
    for head in range(2):
        rows = slice(head * width, (head + 1) * width)
        prompt_scores = jnp.where(visible, nt(prompt_keys, queries[head]), masked_score)
        own_scores = jnp.where(causal, nt(own_keys, queries[head]), masked_score)
        top = jnp.maximum(
            jnp.max(prompt_scores, 0, keepdims=True), jnp.max(own_scores, 0, keepdims=True)
        )
        prompt_exp = jnp.exp(prompt_scores - top)
        own_exp = jnp.exp(own_scores - top)
        total = jnp.sum(prompt_exp, 0, keepdims=True) + jnp.sum(own_exp, 0, keepdims=True)
        summed = nn(prompt_values[rows], prompt_exp.astype(bf16)) + nn(
            own_values[rows], own_exp.astype(bf16)
        )
        mixed.append(summed / total)
        lse_ref[0, head : head + 1, :] = top + jnp.log(total)
    o_ref[...] = jnp.concatenate(mixed, 0).T.astype(bf16)


def attend(seen, qkv, pqkv):
    rows, width = qkv.shape[0], qkv.shape[1] // 3
    count, plen = seen.shape[0], pqkv.shape[0]
    length, head_width, pairs = rows // count, width // HEADS, HEADS // 2
    lanes = 2 * head_width

    def part(size, which, own):
        return pl.BlockSpec(
            (size, lanes), lambda c, p, s: (c if own else 0, p + which * pairs)
        )

    return pl.pallas_call(
        functools.partial(attend_kernel, width=head_width),
        grid_spec=pltpu.PrefetchScalarGridSpec(
            num_scalar_prefetch=1,
            grid=(count, pairs),
            in_specs=[
                part(length, 0, True),
                part(length, 1, True),
                part(length, 2, True),
                part(plen, 1, False),
                part(plen, 2, False),
            ],
            out_specs=[
                part(length, 0, True),
                pl.BlockSpec((1, 2, length), lambda c, p, s: (c * pairs + p, 0, 0)),
            ],
        ),
        out_shape=[
            jax.ShapeDtypeStruct((rows, width), bf16),
            jax.ShapeDtypeStruct((count * pairs, 2, length), f32),
        ],
        cost_estimate=pl.CostEstimate(
            flops=4 * rows * (plen + length) * width,
            bytes_accessed=2 * (4 * rows + 2 * plen) * width,
            transcendentals=rows * (plen + length) * HEADS,
        ),
        name="attend",
    )(seen, qkv, qkv, qkv, pqkv, pqkv)


def attend_back_kernel(
    seen_ref,
    q_ref,
    k_ref,
    v_ref,
    pk_ref,
    pv_ref,
    o_ref,
    lse_ref,
    do_ref,
    carry_ref,
    dqkv_ref,
    dpkv_ref,
    *,
    width,
    pairs,
):
    cont, pair = pl.program_id(0), pl.program_id(1)
    offset = seen_ref[cont]
    length, plen = q_ref.shape[0], pk_ref.shape[0]
    lanes = 2 * width
    queries = head_split(q_ref[...] * bf16(score_scale), width)
    grad = do_ref[...]
    grads = head_split(grad, width)
    prompt_keys, own_keys = pk_ref[...], k_ref[...]
    prompt_values, own_values = pv_ref[...], v_ref[...]
    prompt_turned, own_turned = prompt_keys.T, own_keys.T
    product = (grad.astype(f32) * o_ref[...].astype(f32)).T
    visible = lax.broadcasted_iota(jnp.int32, (plen, length), 0) < offset
    causal = lax.broadcasted_iota(jnp.int32, (length, length), 0) <= lax.broadcasted_iota(
        jnp.int32, (length, length), 1
    )
    dq = []
    dk = dv = dpk = dpv = 0.0
    for head in range(2):
        rows = slice(head * width, (head + 1) * width)
        query, grad_head = queries[head], grads[head]
        delta = jnp.sum(product[rows], 0, keepdims=True)
        lse = lse_ref[0, head : head + 1, :]
        prompt_p = jnp.exp(jnp.where(visible, nt(prompt_keys, query), masked_score) - lse)
        own_p = jnp.exp(jnp.where(causal, nt(own_keys, query), masked_score) - lse)
        prompt_ds = (prompt_p * (nt(prompt_values, grad_head) - delta)).astype(bf16)
        own_ds = (own_p * (nt(own_values, grad_head) - delta)).astype(bf16)
        dpv += nn(prompt_p.astype(bf16), grad_head)
        dv += nn(own_p.astype(bf16), grad_head)
        dpk += nn(prompt_ds, query)
        dk += nn(own_ds, query)
        dq.append(nn(prompt_turned[rows], prompt_ds) + nn(own_turned[rows], own_ds))
    first = pl.multiple_of(pair * lanes, lanes)
    columns = [pl.ds(first + number * pairs * lanes, lanes) for number in range(3)]
    dqkv_ref[:, columns[0]] = (jnp.concatenate(dq, 0).T * score_scale).astype(bf16)
    dqkv_ref[:, columns[1]] = dk.astype(bf16)
    dqkv_ref[:, columns[2]] = dv.astype(bf16)

    @pl.when(cont == 0)
    def _():
        dpkv_ref[:, columns[0]] = carry_ref[:, columns[0]] + dpk
        dpkv_ref[:, columns[1]] = carry_ref[:, columns[1]] + dpv

    @pl.when(cont > 0)
    def _():
        dpkv_ref[:, columns[0]] += dpk
        dpkv_ref[:, columns[1]] += dpv


def attend_back(seen, qkv, pqkv, o, lse, do, carry):
    rows, width = qkv.shape[0], qkv.shape[1] // 3
    count, plen = seen.shape[0], pqkv.shape[0]
    length, head_width, pairs = rows // count, width // HEADS, HEADS // 2
    lanes = 2 * head_width

    def part(size, which, own):
        return pl.BlockSpec(
            (size, lanes), lambda c, p, s: (c if own else 0, p + which * pairs)
        )

    whole = pl.BlockSpec((plen, 2 * width), lambda c, p, s: (0, 0))
    return pl.pallas_call(
        functools.partial(attend_back_kernel, width=head_width, pairs=pairs),
        grid_spec=pltpu.PrefetchScalarGridSpec(
            num_scalar_prefetch=1,
            grid=(count, pairs),
            in_specs=[
                part(length, 0, True),
                part(length, 1, True),
                part(length, 2, True),
                part(plen, 1, False),
                part(plen, 2, False),
                part(length, 0, True),
                pl.BlockSpec((1, 2, length), lambda c, p, s: (c * pairs + p, 0, 0)),
                part(length, 0, True),
                whole,
            ],
            out_specs=[pl.BlockSpec((length, 3 * width), lambda c, p, s: (c, 0)), whole],
        ),
        out_shape=[
            jax.ShapeDtypeStruct((rows, 3 * width), bf16),
            jax.ShapeDtypeStruct((plen, 2 * width), f32),
        ],
        cost_estimate=pl.CostEstimate(
            flops=10 * rows * (plen + length) * width,
            bytes_accessed=2 * (8 * rows + 10 * plen) * width,
            transcendentals=rows * (plen + length) * HEADS,
        ),
        name="attend_back",
    )(seen, qkv, qkv, qkv, pqkv, pqkv, o, lse, do, carry)


def stacked_heads(pair, width):
    return jnp.concatenate(head_split(pair, width), 0)


def unstacked(block, width):
    rows = block.shape[0] // 2
    lane = lax.broadcasted_iota(jnp.int32, (rows, block.shape[1]), 1)
    return jnp.where(lane < width, block[:rows], block[rows:])


def prompt_scores(place_ref, q_ref, k_ref, width):
    rows, plen = q_ref.shape[0], k_ref.shape[0]
    queries = stacked_heads(q_ref[...] * bf16(score_scale), width)
    column = lax.broadcasted_iota(jnp.int32, (plen, 2 * rows), 1)
    query_row = jnp.where(column < rows, column, column - rows) + place_ref[0] * rows
    visible = lax.broadcasted_iota(jnp.int32, (plen, 2 * rows), 0) <= query_row
    return queries, jnp.where(visible, nt(k_ref[...], queries), masked_score)


def prompt_kernel(place_ref, q_ref, k_ref, v_ref, o_ref, lse_ref, *, width):
    queries, scores = prompt_scores(place_ref, q_ref, k_ref, width)
    top = jnp.max(scores, 0, keepdims=True)
    expd = jnp.exp(scores - top)
    total = jnp.sum(expd, 0, keepdims=True)
    mixed = nn(v_ref[...].T, expd.astype(bf16)) / total
    o_ref[...] = unstacked(mixed.T, width).astype(bf16)
    lse_ref[0] = top + jnp.log(total)


def prompt_specs(rows, plen, pairs, lanes):
    return [
        pl.BlockSpec((rows, lanes), lambda p, s: (s[0], p)),
        pl.BlockSpec((plen, lanes), lambda p, s: (0, p + pairs)),
        pl.BlockSpec((plen, lanes), lambda p, s: (0, p + 2 * pairs)),
    ]


def prompt_attend(place, pqkv, rows):
    plen, width = pqkv.shape[0], pqkv.shape[1] // 3
    pairs, head_width = HEADS // 2, width // HEADS
    lanes = 2 * head_width
    return pl.pallas_call(
        functools.partial(prompt_kernel, width=head_width),
        grid_spec=pltpu.PrefetchScalarGridSpec(
            num_scalar_prefetch=1,
            grid=(pairs,),
            in_specs=prompt_specs(rows, plen, pairs, lanes),
            out_specs=[
                pl.BlockSpec((rows, lanes), lambda p, s: (0, p)),
                pl.BlockSpec((1, 1, 2 * rows), lambda p, s: (p, 0, 0)),
            ],
        ),
        out_shape=[
            jax.ShapeDtypeStruct((rows, width), bf16),
            jax.ShapeDtypeStruct((pairs, 1, 2 * rows), f32),
        ],
        cost_estimate=pl.CostEstimate(
            flops=4 * rows * plen * width,
            bytes_accessed=6 * plen * width,
            transcendentals=rows * plen * HEADS,
        ),
        name="prompt_attend",
    )(place, pqkv, pqkv, pqkv)


def prompt_back_kernel(
    place_ref, q_ref, k_ref, v_ref, o_ref, lse_ref, do_ref, carry_k, carry_v, dqkv_ref, *, width, pairs
):
    rows, lanes = q_ref.shape
    first = pl.multiple_of(pl.program_id(0) * lanes, lanes)
    columns = [pl.ds(first + number * pairs * lanes, lanes) for number in range(3)]
    queries, scores = prompt_scores(place_ref, q_ref, k_ref, width)
    grads = stacked_heads(do_ref[...], width)
    output = o_ref[...]
    product = grads.astype(f32) * jnp.concatenate([output, output], 0).astype(f32)
    delta = jnp.sum(product.T, 0, keepdims=True)
    probs = jnp.exp(scores - lse_ref[0])
    ds = (probs * (nt(v_ref[...], grads) - delta)).astype(bf16)
    dqkv_ref[:, columns[2]] = (carry_v[...] + nn(probs.astype(bf16), grads)).astype(bf16)
    dqkv_ref[:, columns[1]] = (carry_k[...] + nn(ds, queries)).astype(bf16)
    turned = nn(k_ref[...].T, ds) * score_scale
    own = pl.ds(pl.multiple_of(place_ref[0] * rows, rows), rows)
    dqkv_ref[:, columns[0]] = jnp.zeros((dqkv_ref.shape[0], lanes), bf16)
    dqkv_ref[own, columns[0]] = unstacked(turned.T, width).astype(bf16)


def prompt_back(place, pqkv, o, lse, do, carry):
    rows, plen, width = o.shape[0], pqkv.shape[0], pqkv.shape[1] // 3
    pairs, head_width = HEADS // 2, width // HEADS
    lanes = 2 * head_width
    own = pl.BlockSpec((rows, lanes), lambda p, s: (0, p))
    keys = pl.BlockSpec((plen, lanes), lambda p, s: (0, p))
    values = pl.BlockSpec((plen, lanes), lambda p, s: (0, p + pairs))
    return pl.pallas_call(
        functools.partial(prompt_back_kernel, width=head_width, pairs=pairs),
        grid_spec=pltpu.PrefetchScalarGridSpec(
            num_scalar_prefetch=1,
            grid=(pairs,),
            in_specs=prompt_specs(rows, plen, pairs, lanes)
            + [own, pl.BlockSpec((1, 1, 2 * rows), lambda p, s: (p, 0, 0)), own, keys, values],
            out_specs=pl.BlockSpec((plen, 3 * width), lambda p, s: (0, 0)),
        ),
        out_shape=jax.ShapeDtypeStruct((plen, 3 * width), bf16),
        cost_estimate=pl.CostEstimate(
            flops=10 * rows * plen * width,
            bytes_accessed=24 * plen * width,
            transcendentals=rows * plen * HEADS,
        ),
        name="prompt_back",
    )(place, pqkv, pqkv, pqkv, o, lse, do, carry, carry)


def normalised(rows):
    centred = rows - jnp.mean(rows, -1, keepdims=True)
    scale = lax.rsqrt(jnp.mean(centred * centred, -1, keepdims=True) + epsilon)
    return centred * scale, scale


def norm(rows, gain, shift):
    return (normalised(rows)[0] * gain + shift).astype(bf16)


def norm_back(rows, gain, grad):
    unit, scale = normalised(rows)
    inner = grad * gain
    spread = inner - jnp.mean(inner, -1, keepdims=True) - unit * jnp.mean(inner * unit, -1, keepdims=True)
    return spread * scale, jnp.sum(grad * unit, 0), jnp.sum(grad, 0)


def gelu(value):
    return 0.5 * value * (1.0 + jnp.tanh(gelu_coeff * (value + gelu_cubic * value * value * value)))


def gelu_slope(value):
    square = value * value
    bent = jnp.tanh(gelu_coeff * value * (1.0 + gelu_cubic * square))
    inner = gelu_coeff * (1.0 + 3.0 * gelu_cubic * square)
    return 0.5 * (1.0 + bent) + 0.5 * value * (1.0 - bent * bent) * inner


def column_sums(block):
    return jnp.sum(block.astype(f32), 0)


def block_output(w, rows, mixed):
    after = rows + nn(mixed, w["out"]) + w["out_bias"]
    normed = norm(after, w["ln2_gain"], w["ln2_bias"])
    hidden = nn(normed, w["fc"]) + w["fc_bias"]
    active = gelu(hidden).astype(bf16)
    result = after + nn(active, w["proj"]) + w["proj_bias"]
    return result, (after, normed, hidden.astype(bf16), active)


def output_backward(w, kept, grad_rows):
    after, normed, hidden, active = kept
    dz = grad_rows.astype(bf16)
    du = (nt(dz, w["proj"]) * gelu_slope(hidden.astype(f32))).astype(bf16)
    grad_in, gain, shift = norm_back(after, w["ln2_gain"], nt(du, w["fc"]))
    grad_after = grad_in + grad_rows
    da = grad_after.astype(bf16)
    do = nt(da, w["out"]).astype(bf16)
    return grad_after, do, (dz, du, da), (gain, shift)


def swap(value, code, axes, total):
    return lax.ppermute(value, axes, [(i, i ^ code) for i in range(total)])


def lay_kernel(place_ref, *refs, codes, widths):
    outs, sems = refs[len(codes) : -1], refs[-1]
    copies = []
    for ref, group in zip(refs, codes):
        for number, code in enumerate(group):
            first = 0
            for out_ref, size in zip(outs, widths):
                source = ref.at[number, :, pl.ds(first, size)] if len(widths) > 1 else ref.at[number]
                copies.append(
                    pltpu.make_async_copy(
                        source, out_ref.at[place_ref[0] ^ code], sems.at[len(copies)]
                    )
                )
                copies[-1].start()
                first += size
    for copy in copies:
        copy.wait()


def lay_out(place, pieces, codes, widths, name):
    total, rows = sum(len(group) for group in codes), pieces[0].shape[1]
    kind = pieces[0].dtype
    return pl.pallas_call(
        functools.partial(lay_kernel, codes=codes, widths=widths),
        in_specs=[pl.BlockSpec(memory_space=pltpu.SMEM)]
        + [pl.BlockSpec(memory_space=pl.ANY)] * len(pieces),
        out_specs=[pl.BlockSpec((total, rows, size), lambda: (0, 0, 0)) for size in widths],
        out_shape=[jax.ShapeDtypeStruct((total, rows, size), kind) for size in widths],
        scratch_shapes=[pltpu.SemaphoreType.DMA((total * len(widths),))],
        cost_estimate=pl.CostEstimate(
            flops=0, bytes_accessed=4 * total * rows * sum(widths), transcendentals=0
        ),
        name=name,
    )(place, *pieces)


def spread_z(parts):
    return [[part[None]] + [swap(part[None], code, ALL, 32) for code in (2, 4, 6)] for part in parts]


def spread_rest(groups, starts, first, second):
    pieces, codes = [], []
    for base, start, one, two in zip(groups, starts, first, second):
        four = [base, swap(base, one, ALL, 32)]
        four += [swap(piece, two, ALL, 32) for piece in four]
        offsets = [0, one, two, one | two]
        pieces += four + [swap(piece, 8, ALL, 32) for piece in four]
        codes += [
            tuple(code | offset | core for code in start) for core in (0, 8) for offset in offsets
        ]
    return pieces, tuple(codes)


def gather_rows(own, place, tree):
    if not tree:
        return lax.all_gather(own, "seq", axis=0, tiled=True)
    pieces = [own[None]] + [swap(own[None], code, "seq", 8) for code in range(1, 8)]
    return lay_rows(pieces, place)


def lay_rows(pieces, place):
    codes = tuple((code,) for code in range(8))
    rows = lay_out(place, pieces, codes, (pieces[0].shape[2],), "lay_rows")[0]
    return rows.reshape(-1, rows.shape[2])


def gather_plain(head, fc, proj, widths):
    joined = lax.all_gather(jnp.concatenate([head, fc], 1), ALL, axis=0)
    parts, first = [], 0
    for size in widths + (fc.shape[1],):
        parts.append(joined[:, :, first : first + size])
        first += size
    return parts + [lax.all_gather(proj, ALL, axis=0)]


def gather_weights(heads, mlps, x_own, flat, place, tree, widths):
    if not tree:
        gathered = [gather_plain(head, fc, proj, widths) for head, (fc, proj) in zip(heads, mlps)]
        return gathered, gather_rows(x_own, place, tree)
    joined = lax.all_gather(heads[0], ALL, axis=0)
    fc, proj = mlps[0]
    rows = [x_own[None]] + [swap(x_own[None], code, "seq", 8) for code in range(1, 8)]
    fc, proj, rows[6] = lax.optimization_barrier((fc, proj, rows[6]))
    parts, first = [], 0
    for size in widths:
        parts.append(joined[:, :, first : first + size])
        first += size
    bases = [jnp.concatenate(group, 0) for group in spread_z([fc, proj])]
    gathered = [None]
    for head, (fc, proj) in zip(heads[1:], mlps[1:]):
        head, fc, proj, bases[0] = lax.optimization_barrier((head, fc, proj, bases[0]))
        gathered.append(gather_plain(head, fc, proj, widths))
    gathered[0] = parts + lay_mlp(bases, flat)
    return gathered, lay_rows(rows, place)


def lay_mlp(groups, flat):
    result = []
    for base, first, second in zip(groups, (16, 1), (1, 16)):
        pieces, codes = spread_rest([base], [(0, 2, 4, 6)], [first], [second])
        result += lay_out(flat, pieces, codes, (base.shape[2],), "lay_mlp")
    return result


def reduce_stages(block, x_first):
    grp, seq = lax.axis_index("grp"), lax.axis_index("seq")
    z = seq // 2
    terms = [block.reshape((2, 2, 4, 2) + block.shape[1:])]

    def picked(axis, index):
        parts = [lax.dynamic_slice_in_dim(term, index, 1, axis) for term in terms]
        return parts, sum(part.astype(f32) for part in parts)

    core, over_x, over_y = (1, 8, grp % 2), (3, 1, seq % 2), (0, 16, grp // 2)
    for axis, code, mine in (core, over_x, over_y) if x_first else (core, over_y, over_x):
        (leaving,) = yield (picked(axis, 1 - mine)[1].astype(bf16),)
        terms = picked(axis, mine)[0] + [swap(leaving, code, ALL, 32)]
    leaving = yield tuple(picked(2, z ^ step)[1].astype(bf16) for step in (1, 2, 3))
    total = picked(2, z)[1]
    for step, part in zip((1, 2, 3), leaving):
        total = total + swap(part, 2 * step, ALL, 32).astype(f32)
    yield total.reshape(block.shape[1:])


def reduce_blocks(block, x_first, tree):
    if not tree:
        return lax.psum_scatter(block, ALL, scatter_dimension=0, tiled=True).astype(f32)[0]
    stages = reduce_stages(block, x_first)
    leaving = next(stages)
    for stage in range(4):
        leaving = stages.send(leaving)
    return leaving


class Gate:
    def __init__(self, blocks):
        self.stages = [reduce_stages(block, x_first) for block, x_first in blocks]
        self.leaving = [next(stage) for stage in self.stages]

    def hold(self, *values):
        values, self.leaving = lax.optimization_barrier((values, self.leaving))
        self.leaving = [stage.send(part) for stage, part in zip(self.stages, self.leaving)]
        return values


def scatter_rows(block, place, tree):
    if not tree:
        return lax.psum_scatter(block, "seq", scatter_dimension=0, tiled=True).astype(f32)
    rows = block.shape[0] // 8
    total = lax.dynamic_slice_in_dim(block, place * rows, rows, 0).astype(f32)
    for code in range(1, 8):
        piece = lax.dynamic_slice_in_dim(block, (place ^ code) * rows, rows, 0)
        total = total + swap(piece, code, "seq", 8).astype(f32)
    return total


SMALL = (
    "ln1_gain",
    "ln1_bias",
    "q_bias",
    "v_bias",
    "out_bias",
    "ln2_gain",
    "ln2_bias",
    "proj_bias",
    "fc_bias",
)


def body(
    x_prompt,
    x_cont,
    thought_pos,
    offsets,
    dy_prompt,
    dy_cont,
    w_qkv,
    w_out,
    w_fc,
    w_proj,
    ln1_gain,
    ln1_bias,
    q_bias,
    v_bias,
    out_bias,
    ln2_gain,
    ln2_bias,
    fc_bias,
    proj_bias,
):
    count, length, width = x_cont.shape
    rows = count * length
    prompt_dev = x_prompt.shape[0]
    plen = prompt_dev * lax.axis_size("seq")
    devices = lax.axis_size("grp") * lax.axis_size("seq")
    place = lax.axis_index("seq")
    place_ref = place.astype(jnp.int32).reshape(1)
    vectors = dict(
        ln1_gain=ln1_gain,
        ln1_bias=ln1_bias,
        q_bias=q_bias,
        v_bias=v_bias,
        out_bias=out_bias,
        ln2_gain=ln2_gain,
        ln2_bias=ln2_bias,
        proj_bias=proj_bias,
        fc_bias=fc_bias,
    )
    out_rows = w_out.shape[1]
    sizes = [vectors[name].shape[1] for name in SMALL]
    tree = (
        lax.axis_size("grp") == 4 and lax.axis_size("seq") == 8 and out_rows % 8 == 0 and prompt_dev % 16 == 0
    )
    flat_ref = (lax.axis_index("grp") * lax.axis_size("seq") + place).astype(jnp.int32).reshape(1)

    small_lanes = -(-sum(sizes) // (128 * out_rows)) * 128
    heads = []
    for layer in range(LAYERS):
        flat = jnp.concatenate([vectors[name][layer] for name in SMALL])
        extra = jnp.pad(flat, (0, out_rows * small_lanes - flat.shape[0])).reshape(out_rows, small_lanes)
        heads.append(jnp.concatenate([w_qkv[layer], w_out[layer], extra], 1))
    gathered, x_all = gather_weights(
        heads,
        [(w_fc[layer], w_proj[layer]) for layer in range(LAYERS)],
        x_prompt,
        flat_ref,
        place_ref,
        tree,
        (3 * width, width, small_lanes),
    )
    weights = []
    for parts in gathered:
        names = ("qkv", "out", "small", "fc", "proj")
        w = {name: part.reshape(-1, part.shape[2]) for name, part in zip(names, parts)}
        share = w.pop("small").reshape(devices, -1)
        first = 0
        for name, size in zip(SMALL, sizes):
            w[name] = share[:, first : first + size].reshape(devices * size).astype(f32)
            first += size
        w["qkv_bias"] = jnp.concatenate([w["q_bias"], jnp.zeros((width,), f32), w["v_bias"]])
        weights.append(w)

    def project(w, normed):
        return (nn(normed, w["qkv"]) + w["qkv_bias"]).astype(bf16)

    prompt_rows = x_prompt.astype(f32)
    prompt_states = []
    for layer in range(LAYERS):
        w = weights[layer]
        if layer == 0:
            all_normed = norm(x_all.astype(f32), w["ln1_gain"], w["ln1_bias"])
        else:
            all_normed = gather_rows(norm(prompt_rows, w["ln1_gain"], w["ln1_bias"]), place_ref, tree)
        pqkv = project(w, all_normed)
        mixed, lse = prompt_attend(place_ref, pqkv, prompt_dev)
        result, kept = block_output(w, prompt_rows, mixed)
        prompt_states.append((prompt_rows, all_normed, pqkv, mixed, lse, kept))
        prompt_rows = result
    prompt_out = prompt_rows

    def pass_forward(current):
        states = []
        for layer in range(LAYERS):
            w = weights[layer]
            normed = norm(current, w["ln1_gain"], w["ln1_bias"])
            qkv = project(w, normed)
            mixed, lse = attend(offsets, qkv, prompt_states[layer][2])
            result, kept = block_output(w, current, mixed)
            states.append((current, normed, qkv, mixed, lse, kept))
            current = result
        return current, states

    inputs = x_cont.astype(f32)
    latent, latent_states = pass_forward(inputs.reshape(rows, width))
    latent = latent.reshape(count, length, width)
    shifted = jnp.concatenate([jnp.zeros((count, 1, width), f32), latent[:, :-1]], 1)
    marked = jnp.any(
        thought_pos[:, :, None] + 1 == lax.broadcasted_iota(jnp.int32, (1, 1, length), 2), 1
    )[:, :, None]
    current, language_states = pass_forward(jnp.where(marked, shifted, inputs).reshape(rows, width))
    cont_out = current.reshape(count, length, width).astype(bf16)

    carries = [jnp.zeros((plen, 2 * width), f32) for layer in range(LAYERS)]

    def attention_backward(layer, state, grad_after, do):
        w = weights[layer]
        before, normed, qkv, mixed, lse, kept = state
        dqkv, carries[layer] = attend_back(
            offsets, qkv, prompt_states[layer][2], mixed, lse, do, carries[layer]
        )
        grad_in, gain, shift = norm_back(before, w["ln1_gain"], nt(dqkv, w["qkv"]))
        return grad_after + grad_in, dqkv, (gain, shift)

    def blocks(left, right):
        return tn(left, right).astype(bf16).reshape(devices, -1, right.shape[1])

    grad = dy_cont.reshape(rows, width)
    language = [None] * LAYERS
    for layer in reversed(range(LAYERS)):
        state = language_states[layer]
        grad_after, do, outer, ln2 = output_backward(weights[layer], state[5], grad)
        grad, dqkv, ln1 = attention_backward(layer, state, grad_after, do)
        language[layer] = (state, outer, dqkv, ln1 + ln2)
    grad_mixed_in = grad.reshape(count, length, width)
    grad = jnp.concatenate(
        [jnp.where(marked, grad_mixed_in, 0.0)[:, 1:], jnp.zeros((count, 1, width), f32)], 1
    ).reshape(rows, width)
    prompt_grad = dy_prompt
    shares, extras = [], []
    for layer in reversed(range(LAYERS)):
        w = weights[layer]
        state = latent_states[layer]
        grad_after, do, outer, ln2 = output_backward(w, state[5], grad)
        before, normed, pqkv, mixed, lse, kept = prompt_states[layer]
        prompt_after, prompt_do, prompt_outer, prompt_ln2 = output_backward(w, kept, prompt_grad)
        spoken, spoken_outer, spoken_dqkv, spoken_sums = language[layer]
        dz = jnp.concatenate([spoken_outer[0], outer[0], prompt_outer[0]], 0)
        du = jnp.concatenate([spoken_outer[1], outer[1], prompt_outer[1]], 0)
        da = jnp.concatenate([spoken_outer[2], outer[2], prompt_outer[2]], 0)
        proj = blocks(jnp.concatenate([spoken[5][3], state[5][3], kept[3]], 0), dz)
        fc = blocks(jnp.concatenate([spoken[5][1], state[5][1], kept[1]], 0), du)
        gate = Gate([(proj, False), (fc, True)]) if tree and layer == 0 else None
        mixed_all = jnp.concatenate([spoken[3], state[3], mixed], 0)
        if gate:
            mixed_all, da = gate.hold(mixed_all, da)
        out = blocks(mixed_all, da)
        if gate:
            out, do = gate.hold(out, do)
        grad, dqkv, ln1 = attention_backward(layer, state, grad_after, do)
        if gate:
            prompt_do, dqkv = gate.hold(prompt_do, dqkv)
        prompt_dqkv = prompt_back(place_ref, pqkv, mixed, lse, prompt_do, carries[layer])
        partial = nt(prompt_dqkv, w["qkv"])
        grad_normed = scatter_rows(partial.astype(bf16), place, tree)
        grad_in, gain, shift = norm_back(before, w["ln1_gain"], grad_normed)
        if layer == 0:
            gain = jnp.sum(partial * normalised(x_all.astype(f32))[0], 0)
            shift = jnp.sum(partial, 0)
        prompt_grad = prompt_after + grad_in
        if gate:
            prompt_dqkv, dqkv = gate.hold(prompt_dqkv, dqkv)
        normed_all = jnp.concatenate([spoken[1], state[1], normed], 0)
        dqkv_all = jnp.concatenate([spoken_dqkv, dqkv, prompt_dqkv], 0)
        qkv = blocks(normed_all, dqkv_all)
        gain1, shift1, gain2, shift2 = [
            sum(parts) for parts in zip(spoken_sums, ln1 + ln2, (gain, shift) + prompt_ln2)
        ]
        qkv_sums = column_sums(dqkv_all)
        vector_grads = dict(
            ln1_gain=gain1,
            ln1_bias=shift1,
            q_bias=qkv_sums[:width],
            v_bias=qkv_sums[2 * width :],
            out_bias=column_sums(da),
            ln2_gain=gain2,
            ln2_bias=shift2,
            proj_bias=column_sums(dz),
            fc_bias=column_sums(du),
        )
        flat = jnp.concatenate(
            [
                vector_grads[name].reshape(devices, size)
                for name, size in zip(SMALL, sizes)
            ],
            1,
        )
        extras.append(
            jnp.pad(flat, ((0, 0), (0, 8 * width - flat.shape[1]))).astype(bf16).reshape(devices, 8, width)
        )

        if layer > 0:
            mlp = proj.reshape(devices, -1, out_rows, width)
            pieces_out = mlp.shape[1]
            packed = jnp.concatenate(
                [qkv, fc, out] + [mlp[:, number] for number in range(pieces_out)], 2
            )
            packed, grad = lax.optimization_barrier((packed, grad))
            total = lax.psum_scatter(packed, ALL, scatter_dimension=0, tiled=True).astype(f32)[0]
            columns = [
                total[:, first * width : last * width]
                for first, last in [(0, 3), (3, 7), (7, 8)] + [(8 + n, 9 + n) for n in range(pieces_out)]
            ]
            result = dict(
                qkv=columns[0], fc=columns[1], out=columns[2], proj=jnp.concatenate(columns[3:], 0)
            )
        else:
            half = 3 * width // 2
            result = {}
            result["proj"], result["fc"] = (
                gate.leaving if gate else (reduce_blocks(proj, False, tree), reduce_blocks(fc, True, tree))
            )
            share = reduce_blocks(jnp.concatenate([out] + extras, 1), False, tree)
            result["qkv"] = jnp.concatenate(
                [
                    reduce_blocks(qkv[:, :, :half], True, tree),
                    reduce_blocks(qkv[:, :, half:], False, tree),
                ],
                1,
            )
            result["out"] = share[:out_rows]
        shares.append(result)
    for number, result in enumerate(shares):
        lines = share[out_rows + 8 * number : out_rows + 8 * (number + 1)].reshape(8 * width)
        first = 0
        for name, size in zip(SMALL, sizes):
            result[name] = lines[first : first + size]
            first += size
    shares.reverse()
    grad_cont = jnp.where(marked, 0.0, grad_mixed_in) + grad.reshape(count, length, width)
    names = ("qkv", "out", "fc", "proj") + (
        "ln1_gain",
        "ln1_bias",
        "q_bias",
        "v_bias",
        "out_bias",
        "ln2_gain",
        "ln2_bias",
        "fc_bias",
        "proj_bias",
    )
    return (prompt_out.astype(bf16), cont_out, prompt_grad, grad_cont) + tuple(
        jnp.stack([shares[layer][name] for layer in range(LAYERS)]) for name in names
    )


def solution(mesh):
    row, cube, matrix, vector = (
        P(ALL, None),
        P(ALL, None, None),
        P(None, ALL, None),
        P(None, ALL),
    )
    return jax.shard_map(
        body,
        mesh=mesh,
        in_specs=(row, cube, row, P(ALL), row, cube) + (matrix,) * 4 + (vector,) * 9,
        out_specs=(row, cube, row, cube) + (matrix,) * 4 + (vector,) * 9,
        check_vma=False,
    )
```

```python
import functools

import jax
import jax.numpy as jnp
from jax import lax
from jax.experimental import pallas as pl
from jax.experimental.pallas import tpu as pltpu
from jax.sharding import PartitionSpec as P

HEADS = 12
LAYERS = 2
epsilon = 1e-05
score_scale = 0.125
gelu_coeff = 0.7978845608028654
gelu_cubic = 0.044715
masked_score = -1e30
ALL = ("grp", "seq")
bf16 = jnp.bfloat16
f32 = jnp.float32


def nn(left, right):
    return lax.dot_general(left, right, (((1,), (0,)), ((), ())), preferred_element_type=f32)


def nt(left, right):
    return lax.dot_general(left, right, (((1,), (1,)), ((), ())), preferred_element_type=f32)


def tn(left, right):
    return lax.dot_general(left, right, (((0,), (0,)), ((), ())), preferred_element_type=f32)


def head_split(pair, width):
    lane = lax.broadcasted_iota(jnp.int32, pair.shape, 1)
    zero = jnp.zeros_like(pair)
    return jnp.where(lane < width, pair, zero), jnp.where(lane >= width, pair, zero)


def attend_kernel(seen_ref, q_ref, k_ref, v_ref, pk_ref, pv_ref, o_ref, lse_ref, *, width):
    offset = seen_ref[pl.program_id(0)]
    length, plen = q_ref.shape[0], pk_ref.shape[0]
    queries = head_split(q_ref[...] * bf16(score_scale), width)
    prompt_keys, own_keys = pk_ref[...], k_ref[...]
    prompt_values, own_values = pv_ref[...].T, v_ref[...].T
    visible = lax.broadcasted_iota(jnp.int32, (plen, length), 0) < offset
    causal = lax.broadcasted_iota(jnp.int32, (length, length), 0) <= lax.broadcasted_iota(
        jnp.int32, (length, length), 1
    )
    mixed = []
    for head in range(2):
        rows = slice(head * width, (head + 1) * width)
        prompt_scores = jnp.where(visible, nt(prompt_keys, queries[head]), masked_score)
        own_scores = jnp.where(causal, nt(own_keys, queries[head]), masked_score)
        top = jnp.maximum(
            jnp.max(prompt_scores, 0, keepdims=True), jnp.max(own_scores, 0, keepdims=True)
        )
        prompt_exp = jnp.exp(prompt_scores - top)
        own_exp = jnp.exp(own_scores - top)
        total = jnp.sum(prompt_exp, 0, keepdims=True) + jnp.sum(own_exp, 0, keepdims=True)
        summed = nn(prompt_values[rows], prompt_exp.astype(bf16)) + nn(
            own_values[rows], own_exp.astype(bf16)
        )
        mixed.append(summed / total)
        lse_ref[0, head : head + 1, :] = top + jnp.log(total)
    o_ref[...] = jnp.concatenate(mixed, 0).T.astype(bf16)


def attend(seen, qkv, pqkv):
    rows, width = qkv.shape[0], qkv.shape[1] // 3
    count, plen = seen.shape[0], pqkv.shape[0]
    length, head_width, pairs = rows // count, width // HEADS, HEADS // 2
    lanes = 2 * head_width

    def part(size, which, own):
        return pl.BlockSpec(
            (size, lanes), lambda c, p, s: (c if own else 0, p + which * pairs)
        )

    return pl.pallas_call(
        functools.partial(attend_kernel, width=head_width),
        grid_spec=pltpu.PrefetchScalarGridSpec(
            num_scalar_prefetch=1,
            grid=(count, pairs),
            in_specs=[
                part(length, 0, True),
                part(length, 1, True),
                part(length, 2, True),
                part(plen, 1, False),
                part(plen, 2, False),
            ],
            out_specs=[
                part(length, 0, True),
                pl.BlockSpec((1, 2, length), lambda c, p, s: (c * pairs + p, 0, 0)),
            ],
        ),
        out_shape=[
            jax.ShapeDtypeStruct((rows, width), bf16),
            jax.ShapeDtypeStruct((count * pairs, 2, length), f32),
        ],
        cost_estimate=pl.CostEstimate(
            flops=4 * rows * (plen + length) * width,
            bytes_accessed=2 * (4 * rows + 2 * plen) * width,
            transcendentals=rows * (plen + length) * HEADS,
        ),
        name="attend",
    )(seen, qkv, qkv, qkv, pqkv, pqkv)


def attend_back_kernel(
    seen_ref,
    q_ref,
    k_ref,
    v_ref,
    pk_ref,
    pv_ref,
    o_ref,
    lse_ref,
    do_ref,
    carry_ref,
    dqkv_ref,
    dpkv_ref,
    *,
    width,
    pairs,
):
    cont, pair = pl.program_id(0), pl.program_id(1)
    offset = seen_ref[cont]
    length, plen = q_ref.shape[0], pk_ref.shape[0]
    lanes = 2 * width
    queries = head_split(q_ref[...] * bf16(score_scale), width)
    grad = do_ref[...]
    grads = head_split(grad, width)
    prompt_keys, own_keys = pk_ref[...], k_ref[...]
    prompt_values, own_values = pv_ref[...], v_ref[...]
    prompt_turned, own_turned = prompt_keys.T, own_keys.T
    product = (grad.astype(f32) * o_ref[...].astype(f32)).T
    visible = lax.broadcasted_iota(jnp.int32, (plen, length), 0) < offset
    causal = lax.broadcasted_iota(jnp.int32, (length, length), 0) <= lax.broadcasted_iota(
        jnp.int32, (length, length), 1
    )
    dq = []
    dk = dv = dpk = dpv = 0.0
    for head in range(2):
        rows = slice(head * width, (head + 1) * width)
        query, grad_head = queries[head], grads[head]
        delta = jnp.sum(product[rows], 0, keepdims=True)
        lse = lse_ref[0, head : head + 1, :]
        prompt_p = jnp.exp(jnp.where(visible, nt(prompt_keys, query), masked_score) - lse)
        own_p = jnp.exp(jnp.where(causal, nt(own_keys, query), masked_score) - lse)
        prompt_ds = (prompt_p * (nt(prompt_values, grad_head) - delta)).astype(bf16)
        own_ds = (own_p * (nt(own_values, grad_head) - delta)).astype(bf16)
        dpv += nn(prompt_p.astype(bf16), grad_head)
        dv += nn(own_p.astype(bf16), grad_head)
        dpk += nn(prompt_ds, query)
        dk += nn(own_ds, query)
        dq.append(nn(prompt_turned[rows], prompt_ds) + nn(own_turned[rows], own_ds))
    first = pl.multiple_of(pair * lanes, lanes)
    columns = [pl.ds(first + number * pairs * lanes, lanes) for number in range(3)]
    dqkv_ref[:, columns[0]] = (jnp.concatenate(dq, 0).T * score_scale).astype(bf16)
    dqkv_ref[:, columns[1]] = dk.astype(bf16)
    dqkv_ref[:, columns[2]] = dv.astype(bf16)

    @pl.when(cont == 0)
    def _():
        dpkv_ref[:, columns[0]] = carry_ref[:, columns[0]] + dpk
        dpkv_ref[:, columns[1]] = carry_ref[:, columns[1]] + dpv

    @pl.when(cont > 0)
    def _():
        dpkv_ref[:, columns[0]] += dpk
        dpkv_ref[:, columns[1]] += dpv


def attend_back(seen, qkv, pqkv, o, lse, do, carry):
    rows, width = qkv.shape[0], qkv.shape[1] // 3
    count, plen = seen.shape[0], pqkv.shape[0]
    length, head_width, pairs = rows // count, width // HEADS, HEADS // 2
    lanes = 2 * head_width

    def part(size, which, own):
        return pl.BlockSpec(
            (size, lanes), lambda c, p, s: (c if own else 0, p + which * pairs)
        )

    whole = pl.BlockSpec((plen, 2 * width), lambda c, p, s: (0, 0))
    return pl.pallas_call(
        functools.partial(attend_back_kernel, width=head_width, pairs=pairs),
        grid_spec=pltpu.PrefetchScalarGridSpec(
            num_scalar_prefetch=1,
            grid=(count, pairs),
            in_specs=[
                part(length, 0, True),
                part(length, 1, True),
                part(length, 2, True),
                part(plen, 1, False),
                part(plen, 2, False),
                part(length, 0, True),
                pl.BlockSpec((1, 2, length), lambda c, p, s: (c * pairs + p, 0, 0)),
                part(length, 0, True),
                whole,
            ],
            out_specs=[pl.BlockSpec((length, 3 * width), lambda c, p, s: (c, 0)), whole],
        ),
        out_shape=[
            jax.ShapeDtypeStruct((rows, 3 * width), bf16),
            jax.ShapeDtypeStruct((plen, 2 * width), f32),
        ],
        cost_estimate=pl.CostEstimate(
            flops=10 * rows * (plen + length) * width,
            bytes_accessed=2 * (8 * rows + 10 * plen) * width,
            transcendentals=rows * (plen + length) * HEADS,
        ),
        name="attend_back",
    )(seen, qkv, qkv, qkv, pqkv, pqkv, o, lse, do, carry)


def stacked_heads(pair, width):
    return jnp.concatenate(head_split(pair, width), 0)


def unstacked(block, width):
    rows = block.shape[0] // 2
    lane = lax.broadcasted_iota(jnp.int32, (rows, block.shape[1]), 1)
    return jnp.where(lane < width, block[:rows], block[rows:])


def prompt_scores(place_ref, q_ref, k_ref, width):
    rows, plen = q_ref.shape[0], k_ref.shape[0]
    queries = stacked_heads(q_ref[...] * bf16(score_scale), width)
    column = lax.broadcasted_iota(jnp.int32, (plen, 2 * rows), 1)
    query_row = jnp.where(column < rows, column, column - rows) + place_ref[0] * rows
    visible = lax.broadcasted_iota(jnp.int32, (plen, 2 * rows), 0) <= query_row
    return queries, jnp.where(visible, nt(k_ref[...], queries), masked_score)


def prompt_kernel(place_ref, q_ref, k_ref, v_ref, o_ref, lse_ref, *, width):
    queries, scores = prompt_scores(place_ref, q_ref, k_ref, width)
    top = jnp.max(scores, 0, keepdims=True)
    expd = jnp.exp(scores - top)
    total = jnp.sum(expd, 0, keepdims=True)
    mixed = nn(v_ref[...].T, expd.astype(bf16)) / total
    o_ref[...] = unstacked(mixed.T, width).astype(bf16)
    lse_ref[0] = top + jnp.log(total)


def prompt_specs(rows, plen, pairs, lanes):
    return [
        pl.BlockSpec((rows, lanes), lambda p, s: (s[0], p)),
        pl.BlockSpec((plen, lanes), lambda p, s: (0, p + pairs)),
        pl.BlockSpec((plen, lanes), lambda p, s: (0, p + 2 * pairs)),
    ]


def prompt_attend(place, pqkv, rows):
    plen, width = pqkv.shape[0], pqkv.shape[1] // 3
    pairs, head_width = HEADS // 2, width // HEADS
    lanes = 2 * head_width
    return pl.pallas_call(
        functools.partial(prompt_kernel, width=head_width),
        grid_spec=pltpu.PrefetchScalarGridSpec(
            num_scalar_prefetch=1,
            grid=(pairs,),
            in_specs=prompt_specs(rows, plen, pairs, lanes),
            out_specs=[
                pl.BlockSpec((rows, lanes), lambda p, s: (0, p)),
                pl.BlockSpec((1, 1, 2 * rows), lambda p, s: (p, 0, 0)),
            ],
        ),
        out_shape=[
            jax.ShapeDtypeStruct((rows, width), bf16),
            jax.ShapeDtypeStruct((pairs, 1, 2 * rows), f32),
        ],
        cost_estimate=pl.CostEstimate(
            flops=4 * rows * plen * width,
            bytes_accessed=6 * plen * width,
            transcendentals=rows * plen * HEADS,
        ),
        name="prompt_attend",
    )(place, pqkv, pqkv, pqkv)


def prompt_back_kernel(
    place_ref, q_ref, k_ref, v_ref, o_ref, lse_ref, do_ref, carry_k, carry_v, dqkv_ref, *, width, pairs
):
    rows, lanes = q_ref.shape
    first = pl.multiple_of(pl.program_id(0) * lanes, lanes)
    columns = [pl.ds(first + number * pairs * lanes, lanes) for number in range(3)]
    queries, scores = prompt_scores(place_ref, q_ref, k_ref, width)
    grads = stacked_heads(do_ref[...], width)
    output = o_ref[...]
    product = grads.astype(f32) * jnp.concatenate([output, output], 0).astype(f32)
    delta = jnp.sum(product.T, 0, keepdims=True)
    probs = jnp.exp(scores - lse_ref[0])
    ds = (probs * (nt(v_ref[...], grads) - delta)).astype(bf16)
    dqkv_ref[:, columns[2]] = (carry_v[...] + nn(probs.astype(bf16), grads)).astype(bf16)
    dqkv_ref[:, columns[1]] = (carry_k[...] + nn(ds, queries)).astype(bf16)
    turned = nn(k_ref[...].T, ds) * score_scale
    own = pl.ds(pl.multiple_of(place_ref[0] * rows, rows), rows)
    dqkv_ref[:, columns[0]] = jnp.zeros((dqkv_ref.shape[0], lanes), bf16)
    dqkv_ref[own, columns[0]] = unstacked(turned.T, width).astype(bf16)


def prompt_back(place, pqkv, o, lse, do, carry):
    rows, plen, width = o.shape[0], pqkv.shape[0], pqkv.shape[1] // 3
    pairs, head_width = HEADS // 2, width // HEADS
    lanes = 2 * head_width
    own = pl.BlockSpec((rows, lanes), lambda p, s: (0, p))
    keys = pl.BlockSpec((plen, lanes), lambda p, s: (0, p))
    values = pl.BlockSpec((plen, lanes), lambda p, s: (0, p + pairs))
    return pl.pallas_call(
        functools.partial(prompt_back_kernel, width=head_width, pairs=pairs),
        grid_spec=pltpu.PrefetchScalarGridSpec(
            num_scalar_prefetch=1,
            grid=(pairs,),
            in_specs=prompt_specs(rows, plen, pairs, lanes)
            + [own, pl.BlockSpec((1, 1, 2 * rows), lambda p, s: (p, 0, 0)), own, keys, values],
            out_specs=pl.BlockSpec((plen, 3 * width), lambda p, s: (0, 0)),
        ),
        out_shape=jax.ShapeDtypeStruct((plen, 3 * width), bf16),
        cost_estimate=pl.CostEstimate(
            flops=10 * rows * plen * width,
            bytes_accessed=24 * plen * width,
            transcendentals=rows * plen * HEADS,
        ),
        name="prompt_back",
    )(place, pqkv, pqkv, pqkv, o, lse, do, carry, carry)


def normalised(rows):
    centred = rows - jnp.mean(rows, -1, keepdims=True)
    scale = lax.rsqrt(jnp.mean(centred * centred, -1, keepdims=True) + epsilon)
    return centred * scale, scale


def norm(rows, gain, shift):
    return (normalised(rows)[0] * gain + shift).astype(bf16)


def norm_back(rows, gain, grad):
    unit, scale = normalised(rows)
    inner = grad * gain
    spread = inner - jnp.mean(inner, -1, keepdims=True) - unit * jnp.mean(inner * unit, -1, keepdims=True)
    return spread * scale, jnp.sum(grad * unit, 0), jnp.sum(grad, 0)


def gelu(value):
    return 0.5 * value * (1.0 + jnp.tanh(gelu_coeff * (value + gelu_cubic * value * value * value)))


def gelu_slope(value):
    square = value * value
    bent = jnp.tanh(gelu_coeff * value * (1.0 + gelu_cubic * square))
    inner = gelu_coeff * (1.0 + 3.0 * gelu_cubic * square)
    return 0.5 * (1.0 + bent) + 0.5 * value * (1.0 - bent * bent) * inner


def column_sums(block):
    return jnp.sum(block.astype(f32), 0)


def block_output(w, rows, mixed):
    after = rows + nn(mixed, w["out"]) + w["out_bias"]
    normed = norm(after, w["ln2_gain"], w["ln2_bias"])
    hidden = nn(normed, w["fc"]) + w["fc_bias"]
    active = gelu(hidden).astype(bf16)
    result = after + nn(active, w["proj"]) + w["proj_bias"]
    return result, (after, normed, hidden.astype(bf16), active)


def output_backward(w, kept, grad_rows):
    after, normed, hidden, active = kept
    dz = grad_rows.astype(bf16)
    du = (nt(dz, w["proj"]) * gelu_slope(hidden.astype(f32))).astype(bf16)
    grad_in, gain, shift = norm_back(after, w["ln2_gain"], nt(du, w["fc"]))
    grad_after = grad_in + grad_rows
    da = grad_after.astype(bf16)
    do = nt(da, w["out"]).astype(bf16)
    return grad_after, do, (dz, du, da), (gain, shift)


def swap(value, code, axes, total):
    return lax.ppermute(value, axes, [(i, i ^ code) for i in range(total)])


def lay_kernel(place_ref, *refs, codes, widths):
    outs, sems = refs[len(codes) : -1], refs[-1]
    copies = []
    for ref, group in zip(refs, codes):
        for number, code in enumerate(group):
            first = 0
            for out_ref, size in zip(outs, widths):
                source = ref.at[number, :, pl.ds(first, size)] if len(widths) > 1 else ref.at[number]
                copies.append(
                    pltpu.make_async_copy(
                        source, out_ref.at[place_ref[0] ^ code], sems.at[len(copies)]
                    )
                )
                copies[-1].start()
                first += size
    for copy in copies:
        copy.wait()


def lay_out(place, pieces, codes, widths, name):
    total, rows = sum(len(group) for group in codes), pieces[0].shape[1]
    kind = pieces[0].dtype
    return pl.pallas_call(
        functools.partial(lay_kernel, codes=codes, widths=widths),
        in_specs=[pl.BlockSpec(memory_space=pltpu.SMEM)]
        + [pl.BlockSpec(memory_space=pl.ANY)] * len(pieces),
        out_specs=[pl.BlockSpec((total, rows, size), lambda: (0, 0, 0)) for size in widths],
        out_shape=[jax.ShapeDtypeStruct((total, rows, size), kind) for size in widths],
        scratch_shapes=[pltpu.SemaphoreType.DMA((total * len(widths),))],
        cost_estimate=pl.CostEstimate(
            flops=0, bytes_accessed=4 * total * rows * sum(widths), transcendentals=0
        ),
        name=name,
    )(place, *pieces)


def spread_z(parts):
    return [[part[None]] + [swap(part[None], code, ALL, 32) for code in (2, 4, 6)] for part in parts]


def spread_rest(groups, starts, first, second):
    pieces, codes = [], []
    for base, start, one, two in zip(groups, starts, first, second):
        four = [base, swap(base, one, ALL, 32)]
        four += [swap(piece, two, ALL, 32) for piece in four]
        offsets = [0, one, two, one | two]
        pieces += four + [swap(piece, 8, ALL, 32) for piece in four]
        codes += [
            tuple(code | offset | core for code in start) for core in (0, 8) for offset in offsets
        ]
    return pieces, tuple(codes)


def gather_rows(own, place, tree):
    if not tree:
        return lax.all_gather(own, "seq", axis=0, tiled=True)
    pieces = [own[None]] + [swap(own[None], code, "seq", 8) for code in range(1, 8)]
    return lay_rows(pieces, place)


def lay_rows(pieces, place):
    codes = tuple((code,) for code in range(8))
    rows = lay_out(place, pieces, codes, (pieces[0].shape[2],), "lay_rows")[0]
    return rows.reshape(-1, rows.shape[2])


def gather_plain(head, fc, proj, widths):
    joined = lax.all_gather(jnp.concatenate([head, fc], 1), ALL, axis=0)
    parts, first = [], 0
    for size in widths + (fc.shape[1],):
        parts.append(joined[:, :, first : first + size])
        first += size
    return parts + [lax.all_gather(proj, ALL, axis=0)]


def gather_weights(heads, mlps, x_own, flat, place, tree, widths):
    if not tree:
        gathered = [gather_plain(head, fc, proj, widths) for head, (fc, proj) in zip(heads, mlps)]
        return gathered, gather_rows(x_own, place, tree)
    joined = lax.all_gather(heads[0], ALL, axis=0)
    fc, proj = mlps[0]
    rows = [x_own[None]] + [swap(x_own[None], code, "seq", 8) for code in range(1, 8)]
    fc, proj, rows[6] = lax.optimization_barrier((fc, proj, rows[6]))
    parts, first = [], 0
    for size in widths:
        parts.append(joined[:, :, first : first + size])
        first += size
    bases = [jnp.concatenate(group, 0) for group in spread_z([fc, proj])]
    gathered = [None]
    for head, (fc, proj) in zip(heads[1:], mlps[1:]):
        head, fc, proj, bases[0] = lax.optimization_barrier((head, fc, proj, bases[0]))
        gathered.append(gather_plain(head, fc, proj, widths))
    gathered[0] = parts + lay_mlp(bases, flat)
    return gathered, lay_rows(rows, place)


def lay_mlp(groups, flat):
    result = []
    for base, first, second in zip(groups, (16, 1), (1, 16)):
        pieces, codes = spread_rest([base], [(0, 2, 4, 6)], [first], [second])
        result += lay_out(flat, pieces, codes, (base.shape[2],), "lay_mlp")
    return result


def reduce_stages(block, x_first):
    grp, seq = lax.axis_index("grp"), lax.axis_index("seq")
    z = seq // 2
    terms = [block.reshape((2, 2, 4, 2) + block.shape[1:])]

    def picked(axis, index):
        parts = [lax.dynamic_slice_in_dim(term, index, 1, axis) for term in terms]
        return parts, sum(part.astype(f32) for part in parts)

    core, over_x, over_y = (1, 8, grp % 2), (3, 1, seq % 2), (0, 16, grp // 2)
    for axis, code, mine in (core, over_x, over_y) if x_first else (core, over_y, over_x):
        (leaving,) = yield (picked(axis, 1 - mine)[1].astype(bf16),)
        terms = picked(axis, mine)[0] + [swap(leaving, code, ALL, 32)]
    leaving = yield tuple(picked(2, z ^ step)[1].astype(bf16) for step in (1, 2, 3))
    total = picked(2, z)[1]
    for step, part in zip((1, 2, 3), leaving):
        total = total + swap(part, 2 * step, ALL, 32).astype(f32)
    yield total.reshape(block.shape[1:])


def reduce_blocks(block, x_first, tree):
    if not tree:
        return lax.psum_scatter(block, ALL, scatter_dimension=0, tiled=True).astype(f32)[0]
    stages = reduce_stages(block, x_first)
    leaving = next(stages)
    for stage in range(4):
        leaving = stages.send(leaving)
    return leaving


class Gate:
    def __init__(self, blocks):
        self.stages = [reduce_stages(block, x_first) for block, x_first in blocks]
        self.leaving = [next(stage) for stage in self.stages]

    def hold(self, *values):
        values, self.leaving = lax.optimization_barrier((values, self.leaving))
        self.leaving = [stage.send(part) for stage, part in zip(self.stages, self.leaving)]
        return values


def scatter_rows(block, place, tree):
    if not tree:
        return lax.psum_scatter(block, "seq", scatter_dimension=0, tiled=True).astype(f32)
    rows = block.shape[0] // 8
    total = lax.dynamic_slice_in_dim(block, place * rows, rows, 0).astype(f32)
    for code in range(1, 8):
        piece = lax.dynamic_slice_in_dim(block, (place ^ code) * rows, rows, 0)
        total = total + swap(piece, code, "seq", 8).astype(f32)
    return total


SMALL = (
    "ln1_gain",
    "ln1_bias",
    "q_bias",
    "v_bias",
    "out_bias",
    "ln2_gain",
    "ln2_bias",
    "proj_bias",
    "fc_bias",
)


def body(
    x_prompt,
    x_cont,
    thought_pos,
    offsets,
    dy_prompt,
    dy_cont,
    w_qkv,
    w_out,
    w_fc,
    w_proj,
    ln1_gain,
    ln1_bias,
    q_bias,
    v_bias,
    out_bias,
    ln2_gain,
    ln2_bias,
    fc_bias,
    proj_bias,
):
    count, length, width = x_cont.shape
    rows = count * length
    prompt_dev = x_prompt.shape[0]
    plen = prompt_dev * lax.axis_size("seq")
    devices = lax.axis_size("grp") * lax.axis_size("seq")
    place = lax.axis_index("seq")
    place_ref = place.astype(jnp.int32).reshape(1)
    vectors = dict(
        ln1_gain=ln1_gain,
        ln1_bias=ln1_bias,
        q_bias=q_bias,
        v_bias=v_bias,
        out_bias=out_bias,
        ln2_gain=ln2_gain,
        ln2_bias=ln2_bias,
        proj_bias=proj_bias,
        fc_bias=fc_bias,
    )
    out_rows = w_out.shape[1]
    sizes = [vectors[name].shape[1] for name in SMALL]
    tree = (
        lax.axis_size("grp") == 4 and lax.axis_size("seq") == 8 and out_rows % 8 == 0 and prompt_dev % 16 == 0
    )
    flat_ref = (lax.axis_index("grp") * lax.axis_size("seq") + place).astype(jnp.int32).reshape(1)

    small_lanes = -(-sum(sizes) // (128 * out_rows)) * 128
    heads = []
    for layer in range(LAYERS):
        flat = jnp.concatenate([vectors[name][layer] for name in SMALL])
        extra = jnp.pad(flat, (0, out_rows * small_lanes - flat.shape[0])).reshape(out_rows, small_lanes)
        heads.append(jnp.concatenate([w_qkv[layer], w_out[layer], extra], 1))
    gathered, x_all = gather_weights(
        heads,
        [(w_fc[layer], w_proj[layer]) for layer in range(LAYERS)],
        x_prompt,
        flat_ref,
        place_ref,
        tree,
        (3 * width, width, small_lanes),
    )
    def unpacked(parts):
        names = ("qkv", "out", "small", "fc", "proj")
        w = {name: part.reshape(-1, part.shape[2]) for name, part in zip(names, parts)}
        share = w.pop("small").reshape(devices, -1)
        first = 0
        for name, size in zip(SMALL, sizes):
            w[name] = share[:, first : first + size].reshape(devices * size).astype(f32)
            first += size
        w["qkv_bias"] = jnp.concatenate([w["q_bias"], jnp.zeros((width,), f32), w["v_bias"]])
        return w

    def project(w, normed):
        return (nn(normed, w["qkv"]) + w["qkv_bias"]).astype(bf16)

    def cont_forward(layer, current):
        w = weights[layer]
        normed = norm(current, w["ln1_gain"], w["ln1_bias"])
        qkv = project(w, normed)
        mixed, lse = attend(offsets, qkv, prompt_states[layer][2])
        result, kept = block_output(w, current, mixed)
        return result, (current, normed, qkv, mixed, lse, kept)

    inputs = x_cont.astype(f32)
    latent = inputs.reshape(rows, width)
    prompt_rows, all_rows = x_prompt.astype(f32), x_all
    weights, prompt_states, latent_states = [], [], []
    for layer in range(LAYERS):
        parts = gathered[layer]
        if layer > 0:
            early, latent = lax.optimization_barrier((parts[:-1], latent))
            parts = list(early) + parts[-1:]
        w = unpacked(parts)
        weights.append(w)
        all_normed = norm(all_rows.astype(f32), w["ln1_gain"], w["ln1_bias"])
        pqkv = project(w, all_normed)
        mixed, lse = prompt_attend(place_ref, pqkv, prompt_dev)
        result, kept = block_output(w, prompt_rows, mixed)
        prompt_states.append((prompt_rows, all_normed, pqkv, mixed, lse, kept))
        prompt_rows = result
        if layer + 1 < LAYERS:
            all_rows = gather_rows(prompt_rows, place_ref, tree)
        latent, state = cont_forward(layer, latent)
        latent_states.append(state)
    prompt_out = prompt_rows
    latent = latent.reshape(count, length, width)
    shifted = jnp.concatenate([jnp.zeros((count, 1, width), f32), latent[:, :-1]], 1)
    marked = jnp.any(
        thought_pos[:, :, None] + 1 == lax.broadcasted_iota(jnp.int32, (1, 1, length), 2), 1
    )[:, :, None]
    current = jnp.where(marked, shifted, inputs).reshape(rows, width)
    language_states = []
    for layer in range(LAYERS):
        current, state = cont_forward(layer, current)
        language_states.append(state)
    cont_out = current.reshape(count, length, width).astype(bf16)

    carries = [jnp.zeros((plen, 2 * width), f32) for layer in range(LAYERS)]

    def attention_backward(layer, state, grad_after, do):
        w = weights[layer]
        before, normed, qkv, mixed, lse, kept = state
        dqkv, carries[layer] = attend_back(
            offsets, qkv, prompt_states[layer][2], mixed, lse, do, carries[layer]
        )
        grad_in, gain, shift = norm_back(before, w["ln1_gain"], nt(dqkv, w["qkv"]))
        return grad_after + grad_in, dqkv, (gain, shift)

    def blocks(left, right):
        return tn(left, right).astype(bf16).reshape(devices, -1, right.shape[1])

    grad = dy_cont.reshape(rows, width)
    language = [None] * LAYERS
    for layer in reversed(range(LAYERS)):
        state = language_states[layer]
        grad_after, do, outer, ln2 = output_backward(weights[layer], state[5], grad)
        grad, dqkv, ln1 = attention_backward(layer, state, grad_after, do)
        language[layer] = (state, outer, dqkv, ln1 + ln2)
    grad_mixed_in = grad.reshape(count, length, width)
    grad = jnp.concatenate(
        [jnp.where(marked, grad_mixed_in, 0.0)[:, 1:], jnp.zeros((count, 1, width), f32)], 1
    ).reshape(rows, width)
    prompt_grad = dy_prompt
    shares, extras = [], []
    for layer in reversed(range(LAYERS)):
        w = weights[layer]
        state = latent_states[layer]
        grad_after, do, outer, ln2 = output_backward(w, state[5], grad)
        before, normed, pqkv, mixed, lse, kept = prompt_states[layer]
        prompt_after, prompt_do, prompt_outer, prompt_ln2 = output_backward(w, kept, prompt_grad)
        spoken, spoken_outer, spoken_dqkv, spoken_sums = language[layer]
        dz = jnp.concatenate([spoken_outer[0], outer[0], prompt_outer[0]], 0)
        du = jnp.concatenate([spoken_outer[1], outer[1], prompt_outer[1]], 0)
        da = jnp.concatenate([spoken_outer[2], outer[2], prompt_outer[2]], 0)
        proj = blocks(jnp.concatenate([spoken[5][3], state[5][3], kept[3]], 0), dz)
        fc = blocks(jnp.concatenate([spoken[5][1], state[5][1], kept[1]], 0), du)
        gate = Gate([(proj, False), (fc, True)]) if tree and layer == 0 else None
        mixed_all = jnp.concatenate([spoken[3], state[3], mixed], 0)
        if gate:
            mixed_all, da = gate.hold(mixed_all, da)
        out = blocks(mixed_all, da)
        if gate:
            out, do = gate.hold(out, do)
        grad, dqkv, ln1 = attention_backward(layer, state, grad_after, do)
        if gate:
            prompt_do, dqkv = gate.hold(prompt_do, dqkv)
        prompt_dqkv = prompt_back(place_ref, pqkv, mixed, lse, prompt_do, carries[layer])
        partial = nt(prompt_dqkv, w["qkv"])
        grad_normed = scatter_rows(partial.astype(bf16), place, tree)
        grad_in, gain, shift = norm_back(before, w["ln1_gain"], grad_normed)
        if layer == 0:
            gain = jnp.sum(partial * normalised(x_all.astype(f32))[0], 0)
            shift = jnp.sum(partial, 0)
        prompt_grad = prompt_after + grad_in
        if gate:
            prompt_dqkv, dqkv = gate.hold(prompt_dqkv, dqkv)
        normed_all = jnp.concatenate([spoken[1], state[1], normed], 0)
        dqkv_all = jnp.concatenate([spoken_dqkv, dqkv, prompt_dqkv], 0)
        qkv = blocks(normed_all, dqkv_all)
        gain1, shift1, gain2, shift2 = [
            sum(parts) for parts in zip(spoken_sums, ln1 + ln2, (gain, shift) + prompt_ln2)
        ]
        qkv_sums = column_sums(dqkv_all)
        vector_grads = dict(
            ln1_gain=gain1,
            ln1_bias=shift1,
            q_bias=qkv_sums[:width],
            v_bias=qkv_sums[2 * width :],
            out_bias=column_sums(da),
            ln2_gain=gain2,
            ln2_bias=shift2,
            proj_bias=column_sums(dz),
            fc_bias=column_sums(du),
        )
        flat = jnp.concatenate(
            [
                vector_grads[name].reshape(devices, size)
                for name, size in zip(SMALL, sizes)
            ],
            1,
        )
        extras.append(
            jnp.pad(flat, ((0, 0), (0, 8 * width - flat.shape[1]))).astype(bf16).reshape(devices, 8, width)
        )

        if layer > 0:
            mlp = proj.reshape(devices, -1, out_rows, width)
            pieces_out = mlp.shape[1]
            packed = jnp.concatenate(
                [qkv, fc, out] + [mlp[:, number] for number in range(pieces_out)], 2
            )
            packed, grad = lax.optimization_barrier((packed, grad))
            total = lax.psum_scatter(packed, ALL, scatter_dimension=0, tiled=True).astype(f32)[0]
            columns = [
                total[:, first * width : last * width]
                for first, last in [(0, 3), (3, 7), (7, 8)] + [(8 + n, 9 + n) for n in range(pieces_out)]
            ]
            result = dict(
                qkv=columns[0], fc=columns[1], out=columns[2], proj=jnp.concatenate(columns[3:], 0)
            )
        else:
            half = 3 * width // 2
            result = {}
            result["proj"], result["fc"] = (
                gate.leaving if gate else (reduce_blocks(proj, False, tree), reduce_blocks(fc, True, tree))
            )
            share = reduce_blocks(jnp.concatenate([out] + extras, 1), False, tree)
            result["qkv"] = jnp.concatenate(
                [
                    reduce_blocks(qkv[:, :, :half], True, tree),
                    reduce_blocks(qkv[:, :, half:], False, tree),
                ],
                1,
            )
            result["out"] = share[:out_rows]
        shares.append(result)
    for number, result in enumerate(shares):
        lines = share[out_rows + 8 * number : out_rows + 8 * (number + 1)].reshape(8 * width)
        first = 0
        for name, size in zip(SMALL, sizes):
            result[name] = lines[first : first + size]
            first += size
    shares.reverse()
    grad_cont = jnp.where(marked, 0.0, grad_mixed_in) + grad.reshape(count, length, width)
    names = ("qkv", "out", "fc", "proj") + (
        "ln1_gain",
        "ln1_bias",
        "q_bias",
        "v_bias",
        "out_bias",
        "ln2_gain",
        "ln2_bias",
        "fc_bias",
        "proj_bias",
    )
    return (prompt_out.astype(bf16), cont_out, prompt_grad, grad_cont) + tuple(
        jnp.stack([shares[layer][name] for layer in range(LAYERS)]) for name in names
    )


def solution(mesh):
    row, cube, matrix, vector = (
        P(ALL, None),
        P(ALL, None, None),
        P(None, ALL, None),
        P(None, ALL),
    )
    return jax.shard_map(
        body,
        mesh=mesh,
        in_specs=(row, cube, row, P(ALL), row, cube) + (matrix,) * 4 + (vector,) * 9,
        out_specs=(row, cube, row, cube) + (matrix,) * 4 + (vector,) * 9,
        check_vma=False,
    )
```
